768 devices in a mesh: sec: 3 (over z_hi), tp: 64 (over z_lo, y, core), blk: 4 (over x).
Axes of the slice: x: 4, y: 8, z: 12 (z_hi: 3, z_lo: 4; z = z_hi * 4 + z_lo), core: 2. Of those that a mesh axis runs over, the one named last changes fastest.
Arguments:
- perambulator: bfloat16 [64, 2, 2048, 2048], P('tp', None, 'blk'), may hold values from -0.125 to 0.125
- backward: bfloat16 [64, 2, 2048, 2048], P('tp', None, None, 'blk'), may hold values from -0.125 to 0.125
- elementals: bfloat16 [3, 64, 2, 2048, 128], P('sec', 'tp', None, 'blk'), may hold values from -6 to 6
- diagrams: int32 [64, 16, 2], P('tp'), may hold values from 0 to 63
- owner_loads: int32 [64], P('tp'), may hold values from 1 to 16, as said below
Outputs:
- hadron: float32 [3, 64, 2, 128, 128], P('sec', 'tp', None, 'blk')
The draws below stay inside these ranges and needn't reach their ends.
Inputs may be any that keep to these rules, and one draw needn't show every extreme that they name: `diagrams`: pair indices of each owner's slots; slots at or past the owner's load are ignored. `owner_loads`: some owner has exactly 16 live slots.
All inputs are finite; a program needn't handle non-finite values.
Results may differ from the reference program's by a relative error of at most 0.007.
Values may be sent and summed in bfloat16 or wider, within the bound.
No kernel may reach another device: no remote copies, remote signals or barrier semaphores. Data moves between devices by JAX's collectives and lax.ppermute only.
A program may use at most 64 MiB of HBM per device.

```python
import jax
import jax.numpy as jnp
from jax import lax

NS = 2048
K = 128
MAXD = 16
PAIRS = 64
DIAGRAM_HOLDERS = 64
INSERTIONS = 3


def draw_owner_loads(key, part):
    first = jax.random.randint(jax.random.fold_in(key, 11), (DIAGRAM_HOLDERS,), 0, MAXD)
    second = jax.random.randint(jax.random.fold_in(key, 12), (DIAGRAM_HOLDERS,), 0, MAXD)
    piece_count = 1 + first * second // MAXD
    where = jax.random.randint(jax.random.fold_in(key, 13), (), 0, DIAGRAM_HOLDERS)
    return piece_count.at[where].set(MAXD).astype(jnp.int32)


def touch_ends(result, own_key, least, top_value):
    extent = result.shape
    index_at = [jax.random.randint(jax.random.fold_in(own_key, axis), (), 0, extent[axis]) for axis in range(len(extent))]
    result = result.at[tuple(index_at)].set(least)
    longest = extent.index(max(extent))
    index_at[longest] = (index_at[longest] + 1) % extent[longest]
    return result.at[tuple(index_at)].set(top_value)


def steps_of(rng, dims, cuts, smallest, top_value):
    gain, own = 1.0, jax.random.fold_in(rng, 6)
    for axis_at, shards_of in cuts:
        draws = jnp.exp(jax.random.uniform(jax.random.fold_in(own, axis_at), (shards_of,), jnp.float32, smallest / len(cuts), top_value / len(cuts)))
        gain = gain * jnp.repeat(draws, dims[axis_at] // shards_of).reshape([-1 if axis == axis_at else 1 for axis in range(len(dims))])
    return gain


def scatter_about(stream_key, dims, spread, limit, cuts=(), dtype=jnp.bfloat16):
    values = jax.random.normal(stream_key, dims, jnp.float32) * spread
    if len(cuts) > 0:
        values = steps_of(stream_key, dims, cuts, -0.22, 0.18) * values
    return jnp.clip(values, min=-limit, max=limit).astype(dtype)


def setup_inputs(seed: int = 0) -> dict:
    splits = jax.random.split(jax.random.key(seed), 6)
    perambulator = scatter_about(splits[0], (PAIRS, 2, NS, NS), NS ** -0.5, 0.125, ((0, 64), (2, 4)))
    backward = scatter_about(splits[1], (PAIRS, 2, NS, NS), NS ** -0.5, 0.125, ((0, 64), (3, 4)))
    elementals = scatter_about(splits[2], (INSERTIONS, PAIRS, 2, NS, K), 1.0, 6.0, ((0, 3), (1, 64), (3, 4)))
    diagrams = touch_ends(jax.random.randint(splits[3], (DIAGRAM_HOLDERS, MAXD, 2), 0, PAIRS), jax.random.fold_in(splits[3], 1), 0, PAIRS - 1).astype(jnp.int32)
    owner_loads = draw_owner_loads(jax.random.fold_in(splits[5], 71), 0)
    return dict(perambulator=perambulator, backward=backward, elementals=elementals, diagrams=diagrams, owner_loads=owner_loads)


def one_pair(pieces):
    peram_pair, back_pair, pair_tiles = pieces
    tau_real = peram_pair[0].astype(jnp.float32)
    tau_imag = peram_pair[1].astype(jnp.float32)
    back_real = back_pair[0].astype(jnp.float32)
    back_imag = back_pair[1].astype(jnp.float32)
    tile_real = pair_tiles[:, 0].astype(jnp.float32)
    tile_imag = pair_tiles[:, 1].astype(jnp.float32)
    image_real = jnp.einsum('rc,sck->srk', tau_real, tile_real) - jnp.einsum('rc,sck->srk', tau_imag, tile_imag)
    image_imag = jnp.einsum('rc,sck->srk', tau_real, tile_imag) + jnp.einsum('rc,sck->srk', tau_imag, tile_real)
    image_real = image_real.astype(jnp.bfloat16).astype(jnp.float32)
    image_imag = image_imag.astype(jnp.bfloat16).astype(jnp.float32)
    dressed_real = jnp.einsum('ri,sik->srk', back_real, image_real) - jnp.einsum('ri,sik->srk', back_imag, image_imag)
    dressed_imag = jnp.einsum('ri,sik->srk', back_real, image_imag) + jnp.einsum('ri,sik->srk', back_imag, image_real)
    dressed_real = dressed_real.astype(jnp.bfloat16).astype(jnp.float32)
    dressed_imag = dressed_imag.astype(jnp.bfloat16).astype(jnp.float32)
    sink_real = jnp.roll(tile_real, 1, axis=0)
    sink_imag = jnp.roll(tile_imag, 1, axis=0)
    norm_scale = NS ** -0.5
    block_real = (jnp.einsum('sjk,sjm->skm', sink_real, dressed_real) + jnp.einsum('sjk,sjm->skm', sink_imag, dressed_imag)) * norm_scale
    block_imag = (jnp.einsum('sjk,sjm->skm', sink_real, dressed_imag) - jnp.einsum('sjk,sjm->skm', sink_imag, dressed_real)) * norm_scale
    return jnp.stack([block_real, block_imag], axis=1).astype(jnp.bfloat16)


def reference(perambulator, backward, elementals, diagrams, owner_loads):
    blocks = lax.map(one_pair, (perambulator, backward, jnp.moveaxis(elementals, 1, 0)))

    def one_owner(pieces):
        owner_list, owner_load = pieces
        left_blocks = jnp.take(blocks, owner_list[:, 0], axis=0)
        right_blocks = jnp.take(blocks, owner_list[:, 1], axis=0)
        active = (jnp.arange(MAXD) < owner_load).astype(jnp.float32)
        left_float = left_blocks.astype(jnp.float32) * active[:, None, None, None, None]
        right_float = right_blocks.astype(jnp.float32)
        hadron_real = jnp.einsum('gsrk,gskm->srm', left_float[:, :, 0], right_float[:, :, 0]) - jnp.einsum('gsrk,gskm->srm', left_float[:, :, 1], right_float[:, :, 1])
        hadron_imag = jnp.einsum('gsrk,gskm->srm', left_float[:, :, 0], right_float[:, :, 1]) + jnp.einsum('gsrk,gskm->srm', left_float[:, :, 1], right_float[:, :, 0])
        return jnp.stack([hadron_real, hadron_imag], axis=1) * ((K * MAXD) ** -0.5)

    hadron = lax.map(one_owner, (diagrams, owner_loads))
    return jnp.moveaxis(hadron, 0, 1)
```

```python
import jax
import jax.numpy as jnp
from jax import lax
from jax.experimental import pallas as pl
from jax.experimental.pallas import tpu as pltpu
from jax.sharding import Mesh
from jax.sharding import PartitionSpec as P

TP = ("z", "y", "c")
BF16 = jnp.bfloat16
F32 = jnp.float32
VMEM = pl.BlockSpec(memory_space=pltpu.VMEM)
SMEM = pl.BlockSpec(memory_space=pltpu.SMEM)


def dot(a, b, ca, cb):
    return lax.dot_general(a, b, (((ca,), (cb,)), ((), ())), preferred_element_type=F32)


def image_kernel(tau_ref, tile_ref, image_ref):
    parts, _, rows, k = tile_ref.shape
    acc_r = acc_i = None
    for j in range(parts):
        both = jnp.concatenate([tile_ref[j, 0], tile_ref[j, 1]], axis=1)
        add_r = dot(tau_ref[0, :, j * rows : (j + 1) * rows], both, 1, 0)
        add_i = dot(tau_ref[1, :, j * rows : (j + 1) * rows], both, 1, 0)
        acc_r = add_r if acc_r is None else acc_r + add_r
        acc_i = add_i if acc_i is None else acc_i + add_i
    image_ref[0] = (acc_r[:, :k] - acc_i[:, k:]).astype(BF16)
    image_ref[1] = (acc_r[:, k:] + acc_i[:, :k]).astype(BF16)


def left_kernel(beta_ref, tile_ref, left_ref):
    parts, _, rows, k = tile_ref.shape
    acc_r = acc_i = None
    for j in range(parts):
        both = jnp.concatenate([tile_ref[j, 0], tile_ref[j, 1]], axis=1)
        add_r = dot(both, beta_ref[0, j * rows : (j + 1) * rows, :], 0, 0)
        add_i = dot(both, beta_ref[1, j * rows : (j + 1) * rows, :], 0, 0)
        acc_r = add_r if acc_r is None else acc_r + add_r
        acc_i = add_i if acc_i is None else acc_i + add_i
    left_ref[0] = (acc_r[:k] + acc_i[k:]).astype(BF16)
    left_ref[1] = (acc_i[:k] - acc_r[k:]).astype(BF16)


def pack_kernel(scale, left_ref, image_ref, meta_ref, out_ref):
    slices = out_ref.shape[0]
    k = image_ref.shape[2]
    both = jnp.concatenate([image_ref[0], image_ref[1]], axis=1)
    from_r = dot(left_ref[0], both, 1, 0)
    from_i = dot(left_ref[1], both, 1, 0)
    real = (from_r[:, :k] - from_i[:, k:]) * scale
    imag = (from_r[:, k:] + from_i[:, :k]) * scale
    cut = [
        x.reshape(slices, k // slices, k) for x in (real.T, imag.T, real, imag)
    ]
    packed = jnp.concatenate(cut, axis=1).astype(BF16)
    n = packed.shape[1]
    out_ref[:, :n, :] = packed
    out_ref[:, n:, :] = jnp.broadcast_to(meta_ref[...][None], (slices, *meta_ref.shape))


def sum_kernel(in_ref, out_ref):
    copies, pairs, rows, _ = out_ref.shape
    parts = in_ref.shape[0] // pairs
    for q in range(pairs):
        total = in_ref[q * parts, :rows, :].astype(F32)
        for j in range(1, parts):
            total = total + in_ref[q * parts + j, :rows, :].astype(F32)
        total = total.astype(BF16)
        for y in range(copies):
            out_ref[y, q] = total


def product_kernel(slots, ny, nc, meta_ref, own_ref, other_ref, out_ref):
    owners = out_ref.shape[0]
    quarters, _, rows, k = out_ref.shape[1:]
    w = own_ref.shape[2] // 4
    for o in range(owners):
        mine = meta_ref[o, 2 * slots + 1]
        load = meta_ref[o, 2 * slots]

        def fetch(p):
            z = p // (ny * nc)
            y = (p // nc) % ny
            here = own_ref[y, z]
            there = other_ref[y, z]
            return jnp.where((p % nc) == mine, here, there).astype(F32)

        lefts, reals, imags = [], [], []
        for g in range(slots):
            left = fetch(meta_ref[o, 2 * g])[: 2 * w]
            right = fetch(meta_ref[o, 2 * g + 1])[2 * w :]
            lefts.append(jnp.where(g < load, left, jnp.zeros_like(left)))
            reals += [right[:w], -right[w:]]
            imags += [right[w:], right[:w]]
        left = jnp.concatenate(lefts, axis=0).astype(BF16)
        right = jnp.concatenate(
            [jnp.concatenate(reals, axis=0), jnp.concatenate(imags, axis=0)], axis=1
        ).astype(BF16)
        both = dot(left, right, 0, 0)
        for q in range(quarters):
            for c in range(2):
                out_ref[o, q, c] = both[q * rows : (q + 1) * rows, c * k : (c + 1) * k].astype(BF16)


def call(kernel, out, specs, name, flops=0, moved=0):
    return pl.pallas_call(
        kernel,
        out_shape=jax.ShapeDtypeStruct(*out),
        in_specs=specs,
        out_specs=VMEM,
        name=name,
        cost_estimate=pl.CostEstimate(flops=flops, bytes_accessed=moved, transcendentals=0),
    )


def on_device(perambulator, backward, elementals, diagrams, owner_loads):
    tau, beta = perambulator[0], backward[0]
    tile = elementals[0, 0]
    _, share, k = tile.shape
    order = tau.shape[2]
    nx, nz, ny, nc = (lax.axis_size(a) for a in ("blk", "z", "y", "c"))
    ns = lax.axis_size("sec")
    slots = diagrams.shape[1]
    slices = nz * nx
    w = k // slices
    quarter = k // nx

    tiles = lax.all_to_all(
        jnp.broadcast_to(tile[None], (nx, *tile.shape)), "blk", 0, 0, tiled=True
    )
    left = call(left_kernel, ((2, k, share), BF16), [VMEM] * 2, "left", 8 * k * order * share, 2**22)(
        beta, tiles
    )
    left = lax.ppermute(left, "sec", [((i - 1) % ns, i) for i in range(ns)])
    image = call(image_kernel, ((2, share, k), BF16), [VMEM] * 2, "image", 8 * k * order * share, 2**22)(
        tau, tiles
    )

    lists = jnp.concatenate([diagrams[0].reshape(-1), owner_loads]).astype(BF16)
    meta = jnp.zeros((16, k), BF16).at[0, : 2 * slots + 1].set(lists)
    packed = call(
        lambda *refs: pack_kernel(order**-0.5, *refs),
        ((slices, 4 * w + 16, k), BF16),
        [VMEM] * 3,
        "pack",
    )(left, image, meta)
    packed = lax.all_to_all(packed, ("z", "blk"), 0, 0, tiled=True)
    pieces = call(sum_kernel, ((ny, nz, 4 * w, k), BF16), [VMEM], "sum")(packed)
    pieces = lax.all_to_all(pieces, "y", 0, 0, tiled=True)
    others = lax.ppermute(pieces, "c", [(i, (i + 1) % nc) for i in range(nc)])

    numbers = packed.reshape(nz, nx, 4 * w + 16, k)[:, 0, 4 * w, :].astype(jnp.int32)
    column = lax.broadcasted_iota(jnp.int32, numbers.shape, 1)
    numbers = jnp.where(column == 2 * slots + 1, lax.axis_index("c"), numbers)
    partial = call(
        lambda *refs: product_kernel(slots, ny, nc, *refs),
        ((nz, nx, 2, quarter, k), BF16),
        [SMEM, VMEM, VMEM],
        "product",
    )(numbers, pieces, others)
    arrived = lax.all_to_all(
        partial.reshape(slices, 2, quarter, k), ("z", "blk"), 0, 0, tiled=True
    )
    total = jnp.sum(arrived.astype(F32), axis=0) * (k * slots) ** (-0.5)
    return total.reshape(1, 1, 2, quarter, k)


def solution(mesh):
    torus = Mesh(
        mesh.devices.reshape(mesh.shape["sec"], 4, 8, 2, mesh.shape["blk"]),
        ("sec", "z", "y", "c", "blk"),
    )
    in_specs = (
        P(TP, None, "blk", None),
        P(TP, None, None, "blk"),
        P("sec", TP, None, "blk", None),
        P(TP, None, None),
        P(TP),
    )
    out_specs = P("sec", TP, None, "blk", None)
    return jax.shard_map(
        on_device, mesh=torus, in_specs=in_specs, out_specs=out_specs, check_vma=False
    )
```

```python
import jax
import jax.numpy as jnp
from jax import lax
from jax.experimental import pallas as pl
from jax.experimental.pallas import tpu as pltpu
from jax.sharding import Mesh
from jax.sharding import PartitionSpec as P

TP = ("z", "y", "c")
BF16 = jnp.bfloat16
F32 = jnp.float32
VMEM = pl.BlockSpec(memory_space=pltpu.VMEM)
SMEM = pl.BlockSpec(memory_space=pltpu.SMEM)
HBM = pl.BlockSpec(memory_space=pltpu.HBM)


def dot(a, b, ca, cb):
    return lax.dot_general(a, b, (((ca,), (cb,)), ((), ())), preferred_element_type=F32)


def swapped(x):
    return pltpu.roll(x, x.shape[-1] // 2, x.ndim - 1)


def lower(x):
    return lax.broadcasted_iota(jnp.int32, x.shape, x.ndim - 1) < x.shape[-1] // 2


def halves_kernel(tile_ref, first_ref, second_ref):
    real = tile_ref[0].astype(F32)
    imag = tile_ref[1].astype(F32)
    first_ref[...] = jnp.where(lower(real), real, swapped(imag)).astype(BF16)
    second = jnp.where(lower(real), swapped(real), imag).astype(BF16)
    for j in range(second_ref.shape[0]):
        second_ref[j] = second


def copies_kernel(own_ref, other_ref, out_ref):
    own, other = own_ref[...], other_ref[...]
    for j in range(out_ref.shape[0]):
        out_ref[j, 0] = own
        out_ref[j, 1] = other


def chunked(source, target, sems, dim, size):
    copies = []
    for j in range(source.shape[dim] // size):
        at = tuple(pl.ds(j * size, size) if d == dim else slice(None) for d in range(3))
        copies.append(pltpu.make_async_copy(source.at[at], target.at[at], sems.at[j]))
        copies[-1].start()
    return copies


def left_half(tile_of, beta_ref, copies):
    acc_r = acc_i = None
    for j, copy in enumerate(copies):
        copy.wait()
        tile = tile_of(j)
        rows = tile.shape[0]
        add_r = dot(tile, beta_ref[0, j * rows : (j + 1) * rows, :], 0, 0)
        add_i = dot(tile, beta_ref[1, j * rows : (j + 1) * rows, :], 0, 0)
        acc_r = add_r if acc_r is None else acc_r + add_r
        acc_i = add_i if acc_i is None else acc_i + add_i
    h = acc_r.shape[0] // 2
    return acc_r[:h] + acc_i[h:], acc_i[:h] - acc_r[h:]


def left_kernel(beta_hbm, tile_ref, left_ref, beta_ref, sems):
    copies = chunked(beta_hbm, beta_ref, sems, 1, tile_ref.shape[1])
    real, imag = left_half(lambda j: tile_ref[j], beta_ref, copies)
    left_ref[0] = real.astype(BF16)
    left_ref[1] = imag.astype(BF16)


def middle_kernel(
    tau_hbm, beta_hbm, first_ref, second_ref, left_ref, image_ref, beta_ref, tau_ref, sems
):
    parts, _, rows, k = first_ref.shape
    beta_copies = chunked(beta_hbm, beta_ref, sems.at[0], 1, rows)
    tau_copies = chunked(tau_hbm, tau_ref, sems.at[1], 2, rows)
    real, imag = left_half(lambda j: first_ref[j, 1], beta_ref, beta_copies)
    left_ref[0] = real.astype(BF16)
    left_ref[1] = imag.astype(BF16)
    acc_r = acc_i = None
    for j in range(parts):
        tau_copies[j].wait()
        both = jnp.concatenate([first_ref[j, 0], second_ref[j]], axis=1)
        add_r = dot(tau_ref[0, :, j * rows : (j + 1) * rows], both, 1, 0)
        add_i = dot(tau_ref[1, :, j * rows : (j + 1) * rows], both, 1, 0)
        acc_r = add_r if acc_r is None else acc_r + add_r
        acc_i = add_i if acc_i is None else acc_i + add_i
    for h in range(2):
        a, b = acc_r[:, h * k : (h + 1) * k], swapped(acc_i[:, h * k : (h + 1) * k])
        image_ref[:, h * k : (h + 1) * k] = (a + jnp.where(lower(b), -b, b)).astype(BF16)


def pack_kernel(scale, lists_ref, load_ref, first_ref, second_ref, image_ref, out_ref):
    slices = out_ref.shape[0]
    k = image_ref.shape[1] // 2
    image = image_ref[...]
    from_r = dot(jnp.concatenate([first_ref[0], second_ref[0]], axis=0), image, 1, 0)
    from_i = dot(jnp.concatenate([first_ref[1], second_ref[1]], axis=0), image, 1, 0)
    halves = []
    for h in range(2):
        a, b = from_r[:, h * k : (h + 1) * k], swapped(from_i[:, h * k : (h + 1) * k])
        halves.append(a + jnp.where(lower(b), -b, b))
    first, second = halves
    real = jnp.where(lower(first), first, swapped(second)) * scale
    imag = jnp.where(lower(first), swapped(first), second) * scale
    cut = [x.reshape(slices, k // slices, k) for x in (real.T, imag.T, real, imag)]
    packed = jnp.concatenate(cut, axis=1).astype(BF16)
    n = packed.shape[1]
    out_ref[:, :n, :] = packed
    sides, slots = lists_ref.shape
    row = lax.broadcasted_iota(jnp.int32, (out_ref.shape[1] - n, k), 0)
    column = lax.broadcasted_iota(jnp.int32, row.shape, 1)
    meta = jnp.where(row == sides, load_ref[0], 0)
    for side in range(sides):
        for g in range(slots):
            meta = jnp.where((row == side) & (column == g), lists_ref[side, g], meta)
    meta = meta.astype(F32).astype(BF16)
    for j in range(slices):
        out_ref[j, n:, :] = meta


def sum_kernel(in_ref, out_ref, numbers_ref):
    copies, pairs, rows, _ = out_ref.shape
    parts = in_ref.shape[0] // pairs
    tail = numbers_ref.shape[1]
    for q in range(pairs):
        total = in_ref[q * parts, :rows, :].astype(F32)
        for j in range(1, parts):
            total = total + in_ref[q * parts + j, :rows, :].astype(F32)
        total = total.astype(BF16)
        for y in range(copies):
            out_ref[y, q] = total
        numbers_ref[q] = in_ref[q * parts, rows:, :].astype(F32).astype(jnp.int32)[:tail]


def product_kernel(slots, ny, nc, scale, numbers_ref, own_ref, other_ref, out_ref):
    owners, quarters, _, rows, k = out_ref.shape
    w = own_ref.shape[2] // 4
    mine = lax.axis_index("c")
    for o in range(owners):
        load = numbers_ref[o, 2, 0]

        def fetch(p, at):
            z = p // (ny * nc)
            y = (p // nc) % ny
            here = own_ref[y, z, at : at + 2 * w, :]
            there = other_ref[y, z, at : at + 2 * w, :]
            return jnp.where((p % nc) == mine, here, there)

        lefts, reals, imags = [], [], []
        for g in range(slots):
            left = fetch(numbers_ref[o, 0, g], 0)
            right = fetch(numbers_ref[o, 1, g], 2 * w).astype(F32)
            lefts.append(jnp.where(g < load, left, jnp.zeros_like(left)))
            reals += [right[:w], -right[w:]]
            imags += [right[w:], right[:w]]
        left = jnp.concatenate(lefts, axis=0)
        right = jnp.concatenate(
            [jnp.concatenate(reals, axis=0), jnp.concatenate(imags, axis=0)], axis=1
        ).astype(BF16)
        both = dot(left, right, 0, 0) * scale
        for q in range(quarters):
            for c in range(2):
                out_ref[o, q, c] = both[q * rows : (q + 1) * rows, c * k : (c + 1) * k].astype(BF16)


def call(kernel, outs, specs, name, scratch=(), flops=0, moved=0, grant=16):
    outs = [jax.ShapeDtypeStruct(*out) for out in outs]
    return pl.pallas_call(
        kernel,
        out_shape=outs,
        in_specs=specs,
        out_specs=[VMEM] * len(outs),
        scratch_shapes=scratch,
        name=name,
        compiler_params=pltpu.CompilerParams(vmem_limit_bytes=grant * 2**20),
        cost_estimate=pl.CostEstimate(flops=flops, bytes_accessed=moved, transcendentals=0),
    )


def on_device(perambulator, backward, elementals, diagrams, owner_loads):
    tau = pltpu.with_memory_space_constraint(perambulator[0], pltpu.HBM)
    beta = pltpu.with_memory_space_constraint(backward[0], pltpu.HBM)
    tile = elementals[0, 0]
    _, share, k = tile.shape
    order = tau.shape[2]
    nx, nz, ny, nc = (lax.axis_size(a) for a in ("blk", "z", "y", "c"))
    ns = lax.axis_size("sec")
    slots = diagrams.shape[1]
    slices = nz * nx
    w = k // slices
    quarter = k // nx
    onward = [((i - 1) % ns, i) for i in range(ns)]
    work = 4 * k * order * share

    first, second = call(
        halves_kernel, [((share, k), BF16), ((nx, share, k), BF16)], [VMEM], "halves"
    )(tile)
    first_before = lax.ppermute(first, "sec", onward)
    seconds = lax.all_to_all(second, "blk", 0, 0, tiled=True)
    (left_second,) = call(
        left_kernel,
        [((2, k // 2, share), BF16)],
        [HBM, VMEM],
        "left",
        [pltpu.VMEM(beta.shape, BF16), pltpu.SemaphoreType.DMA((nx,))],
        work,
        2**22,
        16,
    )(beta, seconds)
    left_second = lax.ppermute(left_second, "sec", onward)
    (copies,) = call(copies_kernel, [((nx, 2, share, k), BF16)], [VMEM] * 2, "copies")(
        first, first_before
    )
    firsts = lax.all_to_all(copies, "blk", 0, 0, tiled=True)
    left_first, image = call(
        middle_kernel,
        [((2, k // 2, share), BF16), ((share, 2 * k), BF16)],
        [HBM, HBM, VMEM, VMEM],
        "middle",
        [
            pltpu.VMEM(beta.shape, BF16),
            pltpu.VMEM(tau.shape, BF16),
            pltpu.SemaphoreType.DMA((2, nx)),
        ],
        3 * work,
        2**23,
        16,
    )(tau, beta, firsts, seconds)

    (packed,) = call(
        lambda *refs: pack_kernel(order**-0.5, *refs),
        [((slices, 4 * w + 16, k), BF16)],
        [SMEM, SMEM, VMEM, VMEM, VMEM],
        "pack",
    )(diagrams[0].T, owner_loads, left_first, left_second, image)
    packed = lax.all_to_all(packed, ("z", "blk"), 0, 0, tiled=True)
    pieces, numbers = call(
        sum_kernel,
        [((ny, nz, 4 * w, k), BF16), ((nz, 8, k), jnp.int32)],
        [VMEM],
        "sum",
    )(packed)
    pieces = lax.all_to_all(pieces, "y", 0, 0, tiled=True)
    others = lax.ppermute(pieces, "c", [(i, (i + 1) % nc) for i in range(nc)])
    (partial,) = call(
        lambda *refs: product_kernel(slots, ny, nc, (k * slots) ** -0.5, *refs),
        [((nz, nx, 2, quarter, k), BF16)],
        [SMEM, VMEM, VMEM],
        "product",
    )(numbers, pieces, others)
    arrived = lax.all_to_all(
        partial.reshape(slices, 2, quarter, k), ("z", "blk"), 0, 0, tiled=True
    )
    total = jnp.sum(arrived.astype(F32), axis=0)
    return total.reshape(1, 1, 2, quarter, k)


def solution(mesh):
    torus = Mesh(
        mesh.devices.reshape(mesh.shape["sec"], 4, 8, 2, mesh.shape["blk"]),
        ("sec", "z", "y", "c", "blk"),
    )
    in_specs = (
        P(TP, None, "blk", None),
        P(TP, None, None, "blk"),
        P("sec", TP, None, "blk", None),
        P(TP, None, None),
        P(TP),
    )
    out_specs = P("sec", TP, None, "blk", None)
    return jax.shard_map(
        on_device, mesh=torus, in_specs=in_specs, out_specs=out_specs, check_vma=False
    )
```

```python
import jax
import jax.numpy as jnp
from jax import lax
from jax.experimental import pallas as pl
from jax.experimental.pallas import tpu as pltpu
from jax.sharding import Mesh
from jax.sharding import PartitionSpec as P


TP = ("z", "y", "c")
BF16 = jnp.bfloat16
F32 = jnp.float32
VMEM = pl.BlockSpec(memory_space=pltpu.VMEM)
SMEM = pl.BlockSpec(memory_space=pltpu.SMEM)
ANY = pl.BlockSpec(memory_space=pl.ANY)
HBM = pl.BlockSpec(memory_space=pltpu.HBM)


def dot(a, b, ca, cb):
    return lax.dot_general(a, b, (((ca,), (cb,)), ((), ())), preferred_element_type=F32)


def swapped(x):
    return pltpu.roll(x, x.shape[-1] // 2, x.ndim - 1)


def lower(x):
    return lax.broadcasted_iota(jnp.int32, x.shape, x.ndim - 1) < x.shape[-1] // 2


def halves_kernel(tile_ref, first_ref, second_ref):
    real = tile_ref[0].astype(F32)
    imag = tile_ref[1].astype(F32)
    first_ref[...] = jnp.where(lower(real), real, swapped(imag)).astype(BF16)
    second = jnp.where(lower(real), swapped(real), imag).astype(BF16)
    for j in range(second_ref.shape[0]):
        second_ref[j] = second


def copies_kernel(own_ref, other_ref, _, out_ref):
    own, other = own_ref[...], other_ref[...]
    for j in range(out_ref.shape[0]):
        out_ref[j, 0] = own
        out_ref[j, 1] = other


def chunked(source, target, sems, dim, size):
    copies = []
    for j in range(source.shape[dim] // size):
        at = tuple(pl.ds(j * size, size) if d == dim else slice(None) for d in range(3))
        copies.append(pltpu.make_async_copy(source.at[at], target.at[at], sems.at[j]))
        copies[-1].start()
    return copies


def left_half(tile_of, beta_ref, copies):
    acc_r = acc_i = None
    for j, copy in enumerate(copies):
        copy.wait()
        tile = tile_of(j)
        rows = tile.shape[0]
        add_r = dot(tile, beta_ref[0, j * rows : (j + 1) * rows, :], 0, 0)
        add_i = dot(tile, beta_ref[1, j * rows : (j + 1) * rows, :], 0, 0)
        acc_r = add_r if acc_r is None else acc_r + add_r
        acc_i = add_i if acc_i is None else acc_i + add_i
    h = acc_r.shape[0] // 2
    return acc_r[:h] + acc_i[h:], acc_i[:h] - acc_r[h:]


def left_kernel(beta_hbm, tile_ref, left_ref, beta_ref, sems):
    copies = chunked(beta_hbm, beta_ref, sems, 1, tile_ref.shape[1])
    real, imag = left_half(lambda j: tile_ref[j], beta_ref, copies)
    left_ref[0] = real.astype(BF16)
    left_ref[1] = imag.astype(BF16)


def middle_kernel(
    tau_hbm, beta_hbm, first_ref, second_ref, left_ref, image_ref, beta_ref, tau_ref, sems
):
    parts, _, rows, k = first_ref.shape
    beta_copies = chunked(beta_hbm, beta_ref, sems.at[0], 1, rows)
    tau_copies = chunked(tau_hbm, tau_ref, sems.at[1], 2, rows)
    real, imag = left_half(lambda j: first_ref[j, 1], beta_ref, beta_copies)
    left_ref[0] = real.astype(BF16)
    left_ref[1] = imag.astype(BF16)
    acc_r = acc_i = None
    for j in range(parts):
        tau_copies[j].wait()
        both = jnp.concatenate([first_ref[j, 0], second_ref[j]], axis=1)
        add_r = dot(tau_ref[0, :, j * rows : (j + 1) * rows], both, 1, 0)
        add_i = dot(tau_ref[1, :, j * rows : (j + 1) * rows], both, 1, 0)
        acc_r = add_r if acc_r is None else acc_r + add_r
        acc_i = add_i if acc_i is None else acc_i + add_i
    for h in range(2):
        a, b = acc_r[:, h * k : (h + 1) * k], swapped(acc_i[:, h * k : (h + 1) * k])
        image_ref[:, h * k : (h + 1) * k] = (a + jnp.where(lower(b), -b, b)).astype(BF16)


def pack_kernel(scale, lists_ref, load_ref, first_ref, second_ref, image_ref, out_ref):
    slices = out_ref.shape[0]
    k = image_ref.shape[1] // 2
    image = image_ref[...]
    from_r = dot(jnp.concatenate([first_ref[0], second_ref[0]], axis=0), image, 1, 0)
    from_i = dot(jnp.concatenate([first_ref[1], second_ref[1]], axis=0), image, 1, 0)
    halves = []
    for h in range(2):
        a, b = from_r[:, h * k : (h + 1) * k], swapped(from_i[:, h * k : (h + 1) * k])
        halves.append(a + jnp.where(lower(b), -b, b))
    first, second = halves
    real = jnp.where(lower(first), first, swapped(second)) * scale
    imag = jnp.where(lower(first), swapped(first), second) * scale
    cut = [x.reshape(slices, k // slices, k) for x in (real.T, imag.T, real, imag)]
    packed = jnp.concatenate(cut, axis=1).astype(BF16)
    n = packed.shape[1]
    out_ref[:, :n, :] = packed
    sides, slots = lists_ref.shape
    row = lax.broadcasted_iota(jnp.int32, (out_ref.shape[1] - n, k), 0)
    column = lax.broadcasted_iota(jnp.int32, row.shape, 1)
    meta = jnp.where(row == sides, load_ref[0], 0)
    for side in range(sides):
        for g in range(slots):
            meta = jnp.where((row == side) & (column == g), lists_ref[side, g], meta)
    meta = meta.astype(F32).astype(BF16)
    for j in range(slices):
        out_ref[j, n:, :] = meta


def sum_kernel(in_ref, out_ref, numbers_ref):
    copies, pairs, rows, _ = out_ref.shape
    parts = in_ref.shape[0] // pairs
    tail = numbers_ref.shape[1]
    for q in range(pairs):
        total = in_ref[q * parts, :rows, :].astype(F32)
        for j in range(1, parts):
            total = total + in_ref[q * parts + j, :rows, :].astype(F32)
        total = total.astype(BF16)
        for y in range(copies):
            out_ref[y, q] = total
        numbers_ref[q] = in_ref[q * parts, rows:, :].astype(F32).astype(jnp.int32)[:tail]


def product_kernel(slots, ny, nc, scale, numbers_ref, own_ref, other_ref, out_ref):
    owners, quarters, _, rows, k = out_ref.shape
    w = own_ref.shape[2] // 4
    mine = lax.axis_index("c")
    for o in range(owners):
        load = numbers_ref[o, 2, 0]

        def fetch(p, at):
            z = p // (ny * nc)
            y = (p // nc) % ny
            here = own_ref[y, z, at : at + 2 * w, :]
            there = other_ref[y, z, at : at + 2 * w, :]
            return jnp.where((p % nc) == mine, here, there)

        lefts, reals, imags = [], [], []
        for g in range(slots):
            left = fetch(numbers_ref[o, 0, g], 0)
            right = fetch(numbers_ref[o, 1, g], 2 * w).astype(F32)
            lefts.append(jnp.where(g < load, left, jnp.zeros_like(left)))
            reals += [right[:w], -right[w:]]
            imags += [right[w:], right[:w]]
        left = jnp.concatenate(lefts, axis=0)
        right = jnp.concatenate(
            [jnp.concatenate(reals, axis=0), jnp.concatenate(imags, axis=0)], axis=1
        ).astype(BF16)
        both = dot(left, right, 0, 0) * scale
        for q in range(quarters):
            for c in range(2):
                out_ref[o, q, c] = both[q * rows : (q + 1) * rows, c * k : (c + 1) * k].astype(BF16)


def call(kernel, outs, specs, scratch=(), flops=0, moved=0, grant=16):
    outs = [jax.ShapeDtypeStruct(*out) for out in outs]
    return pl.pallas_call(
        kernel,
        out_shape=outs,
        in_specs=specs,
        out_specs=[VMEM] * len(outs),
        scratch_shapes=scratch,
        compiler_params=pltpu.CompilerParams(vmem_limit_bytes=grant * 2**20),
        cost_estimate=pl.CostEstimate(flops=flops, bytes_accessed=moved, transcendentals=0),
    )


def on_device(perambulator, backward, elementals, diagrams, owner_loads):
    tau = pltpu.with_memory_space_constraint(perambulator[0], pltpu.HBM)
    beta = pltpu.with_memory_space_constraint(backward[0], pltpu.HBM)
    tile = elementals[0, 0]
    _, share, k = tile.shape
    order = tau.shape[2]
    nx, nz, ny, nc = (lax.axis_size(a) for a in ("blk", "z", "y", "c"))
    ns = lax.axis_size("sec")
    slots = diagrams.shape[1]
    slices = nz * nx
    w = k // slices
    quarter = k // nx
    onward = [((i - 1) % ns, i) for i in range(ns)]
    work = 4 * k * order * share

    first, second = call(halves_kernel, [((share, k), BF16), ((nx, share, k), BF16)], [VMEM])(tile)
    first_before = lax.ppermute(first, "sec", onward)
    seconds = lax.all_to_all(second, "blk", 0, 0, tiled=True)
    (left_second,) = call(
        left_kernel,
        [((2, k // 2, share), BF16)],
        [HBM, VMEM],
        [pltpu.VMEM(beta.shape, BF16), pltpu.SemaphoreType.DMA((nx,))],
        work,
        2**22,
        16,
    )(beta, seconds)
    left_before = lax.ppermute(left_second, "sec", onward)
    (copies,) = call(copies_kernel, [((nx, 2, share, k), BF16)], [VMEM, VMEM, ANY])(
        first, first_before, left_second
    )
    firsts = lax.all_to_all(copies, "blk", 0, 0, tiled=True)
    left_first, image = call(
        middle_kernel,
        [((2, k // 2, share), BF16), ((share, 2 * k), BF16)],
        [HBM, HBM, VMEM, VMEM],
        [
            pltpu.VMEM(beta.shape, BF16),
            pltpu.VMEM(tau.shape, BF16),
            pltpu.SemaphoreType.DMA((2, nx)),
        ],
        3 * work,
        2**23,
        16,
    )(tau, beta, firsts, seconds)

    (packed,) = call(
        lambda *refs: pack_kernel(order**-0.5, *refs),
        [((slices, 4 * w + 16, k), BF16)],
        [SMEM, SMEM, VMEM, VMEM, VMEM],
    )(diagrams[0].T, owner_loads, left_first, left_before, image)
    packed = lax.all_to_all(packed, ("z", "blk"), 0, 0, tiled=True)
    pieces, numbers = call(
        sum_kernel, [((ny, nz, 4 * w, k), BF16), ((nz, 8, k), jnp.int32)], [VMEM]
    )(packed)
    pieces = lax.all_to_all(pieces, "y", 0, 0, tiled=True)
    others = lax.ppermute(pieces, "c", [(i, (i + 1) % nc) for i in range(nc)])
    (partial,) = call(
        lambda *refs: product_kernel(slots, ny, nc, (k * slots) ** -0.5, *refs),
        [((nz, nx, 2, quarter, k), BF16)],
        [SMEM, VMEM, VMEM],
    )(numbers, pieces, others)
    arrived = lax.all_to_all(
        partial.reshape(slices, 2, quarter, k), ("z", "blk"), 0, 0, tiled=True
    )
    total = jnp.sum(arrived.astype(F32), axis=0)
    return total.reshape(1, 1, 2, quarter, k)


def solution(mesh):
    torus = Mesh(
        mesh.devices.reshape(mesh.shape["sec"], 4, 8, 2, mesh.shape["blk"]),
        ("sec", "z", "y", "c", "blk"),
    )
    in_specs = (
        P(TP, None, "blk", None),
        P(TP, None, None, "blk"),
        P("sec", TP, None, "blk", None),
        P(TP, None, None),
        P(TP),
    )
    out_specs = P("sec", TP, None, "blk", None)
    return jax.shard_map(
        on_device, mesh=torus, in_specs=in_specs, out_specs=out_specs, check_vma=False
    )
```

```python
import jax
import jax.numpy as jnp
from jax import lax
from jax.experimental import pallas as pl
from jax.experimental.pallas import tpu as pltpu
from jax.sharding import Mesh
from jax.sharding import PartitionSpec as P


TP = ("z", "y", "c")
BF16 = jnp.bfloat16
F32 = jnp.float32
VMEM = pl.BlockSpec(memory_space=pltpu.VMEM)
SMEM = pl.BlockSpec(memory_space=pltpu.SMEM)
HBM = pl.BlockSpec(memory_space=pltpu.HBM)


def dot(a, b, ca, cb):
    return lax.dot_general(a, b, (((ca,), (cb,)), ((), ())), preferred_element_type=F32)


def spread_kernel(tile_ref, out_ref):
    both = jnp.concatenate([tile_ref[0], tile_ref[1]], axis=1)
    for j in range(out_ref.shape[0]):
        out_ref[j] = both


def chunked(source, target, sems, dim, size):
    copies = []
    for j in range(source.shape[dim] // size):
        at = tuple(pl.ds(j * size, size) if d == dim else slice(None) for d in range(3))
        copies.append(pltpu.make_async_copy(source.at[at], target.at[at], sems.at[j]))
        copies[-1].start()
    return copies


def product(on_real, on_imag):
    k = on_real.shape[1] // 2
    return jnp.concatenate(
        [on_real[:, :k] - on_imag[:, k:], on_real[:, k:] + on_imag[:, :k]], axis=1
    )


def legs_kernel(tau_hbm, beta_hbm, tile_ref, out_ref, tau_ref, beta_ref, sems):
    parts, rows, _ = tile_ref.shape
    tau_copies = chunked(tau_hbm, tau_ref, sems.at[0], 2, rows)
    beta_copies = chunked(beta_hbm, beta_ref, sems.at[1], 1, rows)
    on_real = on_imag = None
    for j in range(parts):
        tau_copies[j].wait()
        add_real = dot(tau_ref[0, :, j * rows : (j + 1) * rows], tile_ref[j], 1, 0)
        add_imag = dot(tau_ref[1, :, j * rows : (j + 1) * rows], tile_ref[j], 1, 0)
        on_real = add_real if on_real is None else on_real + add_real
        on_imag = add_imag if on_imag is None else on_imag + add_imag
    image = product(on_real, on_imag).astype(BF16)
    for j in range(parts):
        beta_copies[j].wait()
        out_ref[j] = product(
            dot(beta_ref[0, j * rows : (j + 1) * rows, :], image, 1, 0),
            dot(beta_ref[1, j * rows : (j + 1) * rows, :], image, 1, 0),
        ).astype(BF16)


def pack_kernel(scale, lists_ref, load_ref, parts_ref, sink_ref, out_ref):
    slices = out_ref.shape[0]
    k = sink_ref.shape[2]
    dressed = parts_ref[0].astype(F32)
    for j in range(1, parts_ref.shape[0]):
        dressed = dressed + parts_ref[j].astype(F32)
    dressed = dressed.astype(BF16)
    both = product(dot(sink_ref[0], dressed, 0, 0), -dot(sink_ref[1], dressed, 0, 0)) * scale
    real, imag = both[:, :k], both[:, k:]
    cut = [x.reshape(slices, k // slices, k) for x in (real.T, imag.T, real, imag)]
    packed = jnp.concatenate(cut, axis=1).astype(BF16)
    n = packed.shape[1]
    out_ref[:, :n, :] = packed
    sides, slots = lists_ref.shape
    row = lax.broadcasted_iota(jnp.int32, (out_ref.shape[1] - n, k), 0)
    column = lax.broadcasted_iota(jnp.int32, row.shape, 1)
    meta = jnp.where(row == sides, load_ref[0], 0)
    for side in range(sides):
        for g in range(slots):
            meta = jnp.where((row == side) & (column == g), lists_ref[side, g], meta)
    meta = meta.astype(F32).astype(BF16)
    for j in range(slices):
        out_ref[j, n:, :] = meta


def sum_kernel(in_ref, out_ref, numbers_ref):
    copies, pairs, rows, _ = out_ref.shape
    parts = in_ref.shape[0] // pairs
    tail = numbers_ref.shape[1]
    for q in range(pairs):
        total = in_ref[q * parts, :rows, :].astype(F32)
        for j in range(1, parts):
            total = total + in_ref[q * parts + j, :rows, :].astype(F32)
        total = total.astype(BF16)
        for y in range(copies):
            out_ref[y, q] = total
        numbers_ref[q] = in_ref[q * parts, rows:, :].astype(F32).astype(jnp.int32)[:tail]


def product_kernel(slots, ny, nc, scale, numbers_ref, own_ref, other_ref, out_ref):
    owners, quarters, _, rows, k = out_ref.shape
    w = own_ref.shape[2] // 4
    mine = lax.axis_index("c")
    for o in range(owners):
        load = numbers_ref[o, 2, 0]

        def fetch(p, at):
            z = p // (ny * nc)
            y = (p // nc) % ny
            here = own_ref[y, z, at : at + 2 * w, :]
            there = other_ref[y, z, at : at + 2 * w, :]
            return jnp.where((p % nc) == mine, here, there)

        lefts, reals, imags = [], [], []
        for g in range(slots):
            left = fetch(numbers_ref[o, 0, g], 0)
            right = fetch(numbers_ref[o, 1, g], 2 * w).astype(F32)
            lefts.append(jnp.where(g < load, left, jnp.zeros_like(left)))
            reals += [right[:w], -right[w:]]
            imags += [right[w:], right[:w]]
        left = jnp.concatenate(lefts, axis=0)
        right = jnp.concatenate(
            [jnp.concatenate(reals, axis=0), jnp.concatenate(imags, axis=0)], axis=1
        ).astype(BF16)
        both = dot(left, right, 0, 0) * scale
        for q in range(quarters):
            for c in range(2):
                out_ref[o, q, c] = both[q * rows : (q + 1) * rows, c * k : (c + 1) * k].astype(BF16)


def call(kernel, outs, specs, scratch=(), flops=0, moved=0, grant=16):
    outs = [jax.ShapeDtypeStruct(*out) for out in outs]
    return pl.pallas_call(
        kernel,
        out_shape=outs,
        in_specs=specs,
        out_specs=[VMEM] * len(outs),
        scratch_shapes=scratch,
        compiler_params=pltpu.CompilerParams(vmem_limit_bytes=grant * 2**20),
        cost_estimate=pl.CostEstimate(flops=flops, bytes_accessed=moved, transcendentals=0),
    )


def on_device(perambulator, backward, elementals, diagrams, owner_loads):
    tau = pltpu.with_memory_space_constraint(perambulator[0], pltpu.HBM)
    beta = pltpu.with_memory_space_constraint(backward[0], pltpu.HBM)
    tile = elementals[0, 0]
    _, share, k = tile.shape
    order = tau.shape[2]
    nx, nz, ny, nc = (lax.axis_size(a) for a in ("blk", "z", "y", "c"))
    ns = lax.axis_size("sec")
    slots = diagrams.shape[1]
    slices = nz * nx
    w = k // slices
    quarter = k // nx

    before = lax.ppermute(tile, "sec", [((i - 1) % ns, i) for i in range(ns)])
    (tiles,) = call(spread_kernel, [((nx, share, 2 * k), BF16)], [VMEM])(tile)
    tiles = lax.all_to_all(tiles, "blk", 0, 0, tiled=True)
    (dressed,) = call(
        legs_kernel,
        [((nx, share, 2 * k), BF16)],
        [HBM, HBM, VMEM],
        [
            pltpu.VMEM(tau.shape, BF16),
            pltpu.VMEM(beta.shape, BF16),
            pltpu.SemaphoreType.DMA((2, nx)),
        ],
        16 * k * order * share,
        2**23,
    )(tau, beta, tiles)
    dressed = lax.all_to_all(dressed, "blk", 0, 0, tiled=True)
    (packed,) = call(
        lambda *refs: pack_kernel(order**-0.5, *refs),
        [((slices, 4 * w + 16, k), BF16)],
        [SMEM, SMEM, VMEM, VMEM],
    )(diagrams[0].T, owner_loads, dressed, before)
    packed = lax.all_to_all(packed, ("z", "blk"), 0, 0, tiled=True)
    pieces, numbers = call(
        sum_kernel, [((ny, nz, 4 * w, k), BF16), ((nz, 8, k), jnp.int32)], [VMEM]
    )(packed)
    pieces = lax.all_to_all(pieces, "y", 0, 0, tiled=True)
    others = lax.ppermute(pieces, "c", [(i, (i + 1) % nc) for i in range(nc)])
    (partial,) = call(
        lambda *refs: product_kernel(slots, ny, nc, (k * slots) ** -0.5, *refs),
        [((nz, nx, 2, quarter, k), BF16)],
        [SMEM, VMEM, VMEM],
    )(numbers, pieces, others)
    arrived = lax.all_to_all(
        partial.reshape(slices, 2, quarter, k), ("z", "blk"), 0, 0, tiled=True
    )
    total = jnp.sum(arrived.astype(F32), axis=0)
    return total.reshape(1, 1, 2, quarter, k)


def solution(mesh):
    torus = Mesh(
        mesh.devices.reshape(mesh.shape["sec"], 4, 8, 2, mesh.shape["blk"]),
        ("sec", "z", "y", "c", "blk"),
    )
    in_specs = (
        P(TP, None, "blk", None),
        P(TP, None, None, "blk"),
        P("sec", TP, None, "blk", None),
        P(TP, None, None),
        P(TP),
    )
    out_specs = P("sec", TP, None, "blk", None)
    return jax.shard_map(
        on_device, mesh=torus, in_specs=in_specs, out_specs=out_specs, check_vma=False
    )
```

```python
import jax
import jax.numpy as jnp
from jax import lax
from jax.experimental import pallas as pl
from jax.experimental.pallas import tpu as pltpu
from jax.sharding import Mesh
from jax.sharding import PartitionSpec as P


TP = ("z", "y", "c")
BF16 = jnp.bfloat16
F32 = jnp.float32
VMEM = pl.BlockSpec(memory_space=pltpu.VMEM)
HBM = pl.BlockSpec(memory_space=pltpu.HBM)
SMEM = pl.BlockSpec(memory_space=pltpu.SMEM)


def dot(a, b, ca, cb):
    return lax.dot_general(a, b, (((ca,), (cb,)), ((), ())), preferred_element_type=F32)


def spread_kernel(
    tile_hbm, lists_hbm, load_ref, out_ref, meta_ref, tile_ref, lists_ref, sems
):
    tile_copy = pltpu.make_async_copy(tile_hbm, tile_ref, sems.at[0])
    lists_copy = pltpu.make_async_copy(lists_hbm, lists_ref, sems.at[1])
    tile_copy.start()
    lists_copy.start()
    lists_copy.wait()
    sides, slots = lists_ref.shape
    lists = lists_ref[...].astype(F32)
    lists = jnp.concatenate([lists, jnp.zeros((sides, meta_ref.shape[1] - slots), F32)], axis=1)
    row = lax.broadcasted_iota(jnp.int32, meta_ref.shape, 0)
    meta = jnp.where(row == sides, load_ref[0], 0).astype(F32)
    for side in range(sides):
        meta = jnp.where(row == side, lists[side : side + 1], meta)
    meta_ref[...] = meta.astype(BF16)
    tile_copy.wait()
    both = jnp.concatenate([tile_ref[0], tile_ref[1]], axis=1)
    for j in range(out_ref.shape[0]):
        out_ref[j] = both


def chunked(source, target, sems, dim, size):
    copies = []
    for j in range(source.shape[dim] // size):
        at = tuple(pl.ds(j * size, size) if d == dim else slice(None) for d in range(3))
        copies.append(pltpu.make_async_copy(source.at[at], target.at[at], sems.at[j]))
        copies[-1].start()
    return copies


def product(on_real, on_imag):
    k = on_real.shape[1] // 2
    return jnp.concatenate(
        [on_real[:, :k] - on_imag[:, k:], on_real[:, k:] + on_imag[:, :k]], axis=1
    )


def legs_kernel(tau_hbm, beta_hbm, tile_ref, out_ref, tau_ref, beta_ref, sems):
    parts, rows, _ = tile_ref.shape
    tau_copies = chunked(tau_hbm, tau_ref, sems.at[0], 2, rows)
    beta_copies = chunked(beta_hbm, beta_ref, sems.at[1], 1, rows)
    on_real = on_imag = None
    for j in range(parts):
        tau_copies[j].wait()
        add_real = dot(tau_ref[0, :, j * rows : (j + 1) * rows], tile_ref[j], 1, 0)
        add_imag = dot(tau_ref[1, :, j * rows : (j + 1) * rows], tile_ref[j], 1, 0)
        on_real = add_real if on_real is None else on_real + add_real
        on_imag = add_imag if on_imag is None else on_imag + add_imag
    image = product(on_real, on_imag).astype(BF16)
    for j in range(parts):
        beta_copies[j].wait()
        out_ref[j] = product(
            dot(beta_ref[0, j * rows : (j + 1) * rows, :], image, 1, 0),
            dot(beta_ref[1, j * rows : (j + 1) * rows, :], image, 1, 0),
        ).astype(BF16)


def pack_kernel(scale, meta_ref, parts_ref, sink_ref, out_ref):
    slices = out_ref.shape[0]
    k = sink_ref.shape[2]
    dressed = parts_ref[0].astype(F32)
    for j in range(1, parts_ref.shape[0]):
        dressed = dressed + parts_ref[j].astype(F32)
    dressed = dressed.astype(BF16)
    both = product(dot(sink_ref[0], dressed, 0, 0), -dot(sink_ref[1], dressed, 0, 0)) * scale
    real, imag = both[:, :k], both[:, k:]
    cut = [x.reshape(slices, k // slices, k) for x in (real.T, imag.T, real, imag)]
    packed = jnp.concatenate(cut, axis=1).astype(BF16)
    n = packed.shape[1]
    out_ref[:, :n, :] = packed
    for j in range(slices):
        out_ref[j, n:, :] = meta_ref[...]


def sum_kernel(ny, nc, in_ref, out_ref, numbers_ref):
    copies, pairs, rows, _ = out_ref.shape
    parts = in_ref.shape[0] // pairs
    tail = numbers_ref.shape[1]
    mine = lax.axis_index("c")
    for q in range(pairs):
        total = in_ref[q * parts, :rows, :].astype(F32)
        for j in range(1, parts):
            total = total + in_ref[q * parts + j, :rows, :].astype(F32)
        total = total.astype(BF16)
        for y in range(copies):
            out_ref[y, q] = total
        raw = in_ref[q * parts, rows:, :].astype(F32).astype(jnp.int32)[:tail]
        core, rest = raw & (nc - 1), raw >> (nc.bit_length() - 1)
        y, z = rest & (ny - 1), rest >> (ny.bit_length() - 1)
        place = jnp.where(core == mine, 0, ny * pairs) + y * pairs + z
        row = lax.broadcasted_iota(jnp.int32, raw.shape, 0)
        numbers_ref[q] = jnp.where(row < 2, place, raw)


def product_kernel(slots, scale, numbers_ref, own_ref, other_ref, out_ref, both_ref):
    owners, quarters, _, rows, k = out_ref.shape
    n = own_ref.shape[0]
    w = own_ref.shape[1] // 4
    both_ref[:n] = own_ref[...]
    both_ref[n:] = other_ref[...]
    for o in range(owners):
        load = numbers_ref[o, 2, 0]
        lefts, reals, imags = [], [], []
        for g in range(slots):
            left = both_ref[numbers_ref[o, 0, g], : 2 * w, :]
            right = both_ref[numbers_ref[o, 1, g], 2 * w :, :].astype(F32)
            lefts.append(jnp.where(g < load, left, jnp.zeros_like(left)))
            reals += [right[:w], -right[w:]]
            imags += [right[w:], right[:w]]
        left = jnp.concatenate(lefts, axis=0)
        right = jnp.concatenate(
            [jnp.concatenate(reals, axis=0), jnp.concatenate(imags, axis=0)], axis=1
        ).astype(BF16)
        total = dot(left, right, 0, 0) * scale
        for q in range(quarters):
            for c in range(2):
                out_ref[o, q, c] = total[q * rows : (q + 1) * rows, c * k : (c + 1) * k].astype(BF16)


def call(kernel, outs, specs, scratch=(), flops=0, moved=0, grant=16):
    outs = [jax.ShapeDtypeStruct(*out) for out in outs]
    return pl.pallas_call(
        kernel,
        out_shape=outs,
        in_specs=specs,
        out_specs=[VMEM] * len(outs),
        scratch_shapes=scratch,
        compiler_params=pltpu.CompilerParams(vmem_limit_bytes=grant * 2**20),
        cost_estimate=pl.CostEstimate(flops=flops, bytes_accessed=moved, transcendentals=0),
    )


def on_device(perambulator, backward, elementals, diagrams, owner_loads):
    tau = pltpu.with_memory_space_constraint(perambulator[0], pltpu.HBM)
    beta = pltpu.with_memory_space_constraint(backward[0], pltpu.HBM)
    tile = elementals[0, 0]
    lists = diagrams[0].T
    _, share, k = tile.shape
    order = tau.shape[2]
    nx, nz, ny, nc = (lax.axis_size(a) for a in ("blk", "z", "y", "c"))
    ns = lax.axis_size("sec")
    slots = diagrams.shape[1]
    slices = nz * nx
    w = k // slices
    quarter = k // nx

    before = lax.ppermute(tile, "sec", [((i - 1) % ns, i) for i in range(ns)])
    tiles, meta = call(
        spread_kernel,
        [((nx, share, 2 * k), BF16), ((16, k), BF16)],
        [HBM, HBM, SMEM],
        [
            pltpu.VMEM(tile.shape, BF16),
            pltpu.VMEM(lists.shape, jnp.int32),
            pltpu.SemaphoreType.DMA((2,)),
        ],
    )(
        pltpu.with_memory_space_constraint(tile, pltpu.HBM),
        pltpu.with_memory_space_constraint(lists, pltpu.HBM),
        owner_loads,
    )
    tiles = lax.all_to_all(tiles, "blk", 0, 0, tiled=True)
    (dressed,) = call(
        legs_kernel,
        [((nx, share, 2 * k), BF16)],
        [HBM, HBM, VMEM],
        [
            pltpu.VMEM(tau.shape, BF16),
            pltpu.VMEM(beta.shape, BF16),
            pltpu.SemaphoreType.DMA((2, nx)),
        ],
        16 * k * order * share,
        2**23,
    )(tau, beta, tiles)
    dressed = lax.all_to_all(dressed, "blk", 0, 0, tiled=True)
    (packed,) = call(
        lambda *refs: pack_kernel(order**-0.5, *refs), [((slices, 4 * w + 16, k), BF16)], [VMEM] * 3
    )(meta, dressed, before)
    packed = lax.all_to_all(packed, ("z", "blk"), 0, 0, tiled=True)
    pieces, numbers = call(
        lambda *refs: sum_kernel(ny, nc, *refs),
        [((ny, nz, 4 * w, k), BF16), ((nz, 8, k), jnp.int32)],
        [VMEM],
    )(packed)
    pieces = lax.all_to_all(pieces, "y", 0, 0, tiled=True)
    others = lax.ppermute(pieces, "c", [(i, (i + 1) % nc) for i in range(nc)])
    (partial,) = call(
        lambda *refs: product_kernel(slots, (k * slots) ** -0.5, *refs),
        [((nz, nx, 2, quarter, k), BF16)],
        [SMEM, VMEM, VMEM],
        [pltpu.VMEM((2 * ny * nz, 4 * w, k), BF16)],
    )(numbers, *(x.reshape(ny * nz, 4 * w, k) for x in (pieces, others)))
    arrived = lax.all_to_all(
        partial.reshape(slices, 2, quarter, k), ("z", "blk"), 0, 0, tiled=True
    )
    total = jnp.sum(arrived.astype(F32), axis=0)
    return total.reshape(1, 1, 2, quarter, k)


def solution(mesh):
    torus = Mesh(
        mesh.devices.reshape(mesh.shape["sec"], 4, 8, 2, mesh.shape["blk"]),
        ("sec", "z", "y", "c", "blk"),
    )
    in_specs = (
        P(TP, None, "blk", None),
        P(TP, None, None, "blk"),
        P("sec", TP, None, "blk", None),
        P(TP, None, None),
        P(TP),
    )
    out_specs = P("sec", TP, None, "blk", None)
    return jax.shard_map(
        on_device, mesh=torus, in_specs=in_specs, out_specs=out_specs, check_vma=False
    )
```

```python
import jax
import jax.numpy as jnp
from jax import lax
from jax.experimental import pallas as pl
from jax.experimental.pallas import tpu as pltpu
from jax.sharding import Mesh
from jax.sharding import PartitionSpec as P


TP = ("z", "y", "c")
BF16 = jnp.bfloat16
F32 = jnp.float32
VMEM = pl.BlockSpec(memory_space=pltpu.VMEM)
HBM = pl.BlockSpec(memory_space=pltpu.HBM)
SMEM = pl.BlockSpec(memory_space=pltpu.SMEM)


def dot(a, b, ca, cb):
    return lax.dot_general(a, b, (((ca,), (cb,)), ((), ())), preferred_element_type=F32)


def spread_kernel(tile_hbm, out_ref, tile_ref, sem):
    copy = pltpu.make_async_copy(tile_hbm, tile_ref, sem)
    copy.start()
    copy.wait()
    both = jnp.concatenate([tile_ref[0], tile_ref[1]], axis=1)
    for j in range(out_ref.shape[0]):
        out_ref[j] = both


def chunked(source, target, sems, dim, size):
    copies = []
    for j in range(source.shape[dim] // size):
        at = tuple(pl.ds(j * size, size) if d == dim else slice(None) for d in range(3))
        copies.append(pltpu.make_async_copy(source.at[at], target.at[at], sems.at[j]))
        copies[-1].start()
    return copies


def product(on_real, on_imag):
    k = on_real.shape[1] // 2
    return jnp.concatenate(
        [on_real[:, :k] - on_imag[:, k:], on_real[:, k:] + on_imag[:, :k]], axis=1
    )


def legs_kernel(
    tau_hbm,
    beta_hbm,
    tile_ref,
    lists_hbm,
    load_ref,
    out_ref,
    meta_ref,
    tau_ref,
    beta_ref,
    lists_ref,
    sems,
    lists_sem,
):
    parts, rows, _ = tile_ref.shape
    lists_copy = pltpu.make_async_copy(lists_hbm, lists_ref, lists_sem)
    tau_copies = chunked(tau_hbm, tau_ref, sems.at[0], 2, rows)
    beta_copies = chunked(beta_hbm, beta_ref, sems.at[1], 1, rows)
    lists_copy.start()
    on_real = on_imag = None
    for j in range(parts):
        tau_copies[j].wait()
        add_real = dot(tau_ref[0, :, j * rows : (j + 1) * rows], tile_ref[j], 1, 0)
        add_imag = dot(tau_ref[1, :, j * rows : (j + 1) * rows], tile_ref[j], 1, 0)
        on_real = add_real if on_real is None else on_real + add_real
        on_imag = add_imag if on_imag is None else on_imag + add_imag
    image = product(on_real, on_imag).astype(BF16)
    for j in range(parts):
        beta_copies[j].wait()
        out_ref[j] = product(
            dot(beta_ref[0, j * rows : (j + 1) * rows, :], image, 1, 0),
            dot(beta_ref[1, j * rows : (j + 1) * rows, :], image, 1, 0),
        ).astype(BF16)
    lists_copy.wait()
    sides, slots = lists_ref.shape
    lists = lists_ref[...].astype(F32)
    lists = jnp.concatenate([lists, jnp.zeros((sides, meta_ref.shape[1] - slots), F32)], axis=1)
    row = lax.broadcasted_iota(jnp.int32, meta_ref.shape, 0)
    meta = jnp.where(row == sides, load_ref[0], 0).astype(F32)
    for side in range(sides):
        meta = jnp.where(row == side, lists[side : side + 1], meta)
    meta_ref[...] = meta.astype(BF16)


def pack_kernel(scale, meta_ref, parts_ref, sink_ref, out_ref):
    slices = out_ref.shape[0]
    k = sink_ref.shape[2]
    dressed = parts_ref[0].astype(F32)
    for j in range(1, parts_ref.shape[0]):
        dressed = dressed + parts_ref[j].astype(F32)
    dressed = dressed.astype(BF16)
    both = product(dot(sink_ref[0], dressed, 0, 0), -dot(sink_ref[1], dressed, 0, 0)) * scale
    real, imag = both[:, :k], both[:, k:]
    cut = [x.reshape(slices, k // slices, k) for x in (real.T, imag.T, real, imag)]
    packed = jnp.concatenate(cut, axis=1).astype(BF16)
    n = packed.shape[1]
    out_ref[:, :n, :] = packed
    for j in range(slices):
        out_ref[j, n:, :] = meta_ref[...]


def sum_kernel(ny, nc, in_ref, out_ref, numbers_ref):
    copies, pairs, rows, _ = out_ref.shape
    parts = in_ref.shape[0] // pairs
    tail = numbers_ref.shape[1]
    mine = lax.axis_index("c")
    for q in range(pairs):
        total = in_ref[q * parts, :rows, :].astype(F32)
        for j in range(1, parts):
            total = total + in_ref[q * parts + j, :rows, :].astype(F32)
        total = total.astype(BF16)
        for y in range(copies):
            out_ref[y, q] = total
        raw = in_ref[q * parts, rows:, :].astype(F32).astype(jnp.int32)[:tail]
        core, rest = raw & (nc - 1), raw >> (nc.bit_length() - 1)
        y, z = rest & (ny - 1), rest >> (ny.bit_length() - 1)
        place = jnp.where(core == mine, 0, ny * pairs) + y * pairs + z
        row = lax.broadcasted_iota(jnp.int32, raw.shape, 0)
        numbers_ref[q] = jnp.where(row < 2, place, raw)


def product_kernel(slots, scale, numbers_ref, own_ref, other_ref, out_ref, both_ref):
    owners, quarters, _, rows, k = out_ref.shape
    n = own_ref.shape[0]
    w = own_ref.shape[1] // 4
    both_ref[:n] = own_ref[...]
    both_ref[n:] = other_ref[...]
    for o in range(owners):
        load = numbers_ref[o, 2, 0]
        lefts, reals, imags = [], [], []
        for g in range(slots):
            left = both_ref[numbers_ref[o, 0, g], : 2 * w, :]
            right = both_ref[numbers_ref[o, 1, g], 2 * w :, :].astype(F32)
            lefts.append(jnp.where(g < load, left, jnp.zeros_like(left)))
            reals += [right[:w], -right[w:]]
            imags += [right[w:], right[:w]]
        left = jnp.concatenate(lefts, axis=0)
        right = jnp.concatenate(
            [jnp.concatenate(reals, axis=0), jnp.concatenate(imags, axis=0)], axis=1
        ).astype(BF16)
        total = dot(left, right, 0, 0) * scale
        for q in range(quarters):
            for c in range(2):
                out_ref[o, q, c] = total[q * rows : (q + 1) * rows, c * k : (c + 1) * k].astype(BF16)


def call(kernel, outs, specs, scratch=(), flops=0, moved=0, grant=16):
    outs = [jax.ShapeDtypeStruct(*out) for out in outs]
    return pl.pallas_call(
        kernel,
        out_shape=outs,
        in_specs=specs,
        out_specs=[VMEM] * len(outs),
        scratch_shapes=scratch,
        compiler_params=pltpu.CompilerParams(vmem_limit_bytes=grant * 2**20),
        cost_estimate=pl.CostEstimate(flops=flops, bytes_accessed=moved, transcendentals=0),
    )


def on_device(perambulator, backward, elementals, diagrams, owner_loads):
    tau = pltpu.with_memory_space_constraint(perambulator[0], pltpu.HBM)
    beta = pltpu.with_memory_space_constraint(backward[0], pltpu.HBM)
    lists = pltpu.with_memory_space_constraint(diagrams[0].T, pltpu.HBM)
    tile = elementals[0, 0]
    _, share, k = tile.shape
    order = tau.shape[2]
    nx, nz, ny, nc = (lax.axis_size(a) for a in ("blk", "z", "y", "c"))
    ns = lax.axis_size("sec")
    slots = diagrams.shape[1]
    slices = nz * nx
    w = k // slices
    quarter = k // nx

    before = lax.ppermute(tile, "sec", [((i - 1) % ns, i) for i in range(ns)])
    (tiles,) = call(
        spread_kernel,
        [((nx, share, 2 * k), BF16)],
        [HBM],
        [pltpu.VMEM(tile.shape, BF16), pltpu.SemaphoreType.DMA(())],
    )(pltpu.with_memory_space_constraint(tile, pltpu.HBM))
    tiles = lax.all_to_all(tiles, "blk", 0, 0, tiled=True)
    dressed, meta = call(
        legs_kernel,
        [((nx, share, 2 * k), BF16), ((16, k), BF16)],
        [HBM, HBM, VMEM, HBM, SMEM],
        [
            pltpu.VMEM(tau.shape, BF16),
            pltpu.VMEM(beta.shape, BF16),
            pltpu.VMEM(lists.shape, jnp.int32),
            pltpu.SemaphoreType.DMA((2, nx)),
            pltpu.SemaphoreType.DMA(()),
        ],
        16 * k * order * share,
        2**23,
    )(tau, beta, tiles, lists, owner_loads)
    dressed = lax.all_to_all(dressed, "blk", 0, 0, tiled=True)
    (packed,) = call(
        lambda *refs: pack_kernel(order**-0.5, *refs), [((slices, 4 * w + 16, k), BF16)], [VMEM] * 3
    )(meta, dressed, before)
    packed = lax.all_to_all(packed, ("z", "blk"), 0, 0, tiled=True)
    pieces, numbers = call(
        lambda *refs: sum_kernel(ny, nc, *refs),
        [((ny, nz, 4 * w, k), BF16), ((nz, 8, k), jnp.int32)],
        [VMEM],
    )(packed)
    pieces = lax.all_to_all(pieces, "y", 0, 0, tiled=True)
    others = lax.ppermute(pieces, "c", [(i, (i + 1) % nc) for i in range(nc)])
    (partial,) = call(
        lambda *refs: product_kernel(slots, (k * slots) ** -0.5, *refs),
        [((nz, nx, 2, quarter, k), BF16)],
        [SMEM, VMEM, VMEM],
        [pltpu.VMEM((2 * ny * nz, 4 * w, k), BF16)],
    )(numbers, *(x.reshape(ny * nz, 4 * w, k) for x in (pieces, others)))
    arrived = lax.all_to_all(
        partial.reshape(slices, 2, quarter, k), ("z", "blk"), 0, 0, tiled=True
    )
    total = jnp.sum(arrived.astype(F32), axis=0)
    return total.reshape(1, 1, 2, quarter, k)


def solution(mesh):
    torus = Mesh(
        mesh.devices.reshape(mesh.shape["sec"], 4, 8, 2, mesh.shape["blk"]),
        ("sec", "z", "y", "c", "blk"),
    )
    in_specs = (
        P(TP, None, "blk", None),
        P(TP, None, None, "blk"),
        P("sec", TP, None, "blk", None),
        P(TP, None, None),
        P(TP),
    )
    out_specs = P("sec", TP, None, "blk", None)
    return jax.shard_map(
        on_device, mesh=torus, in_specs=in_specs, out_specs=out_specs, check_vma=False
    )
```

```python
import jax
import jax.numpy as jnp
from jax import lax
from jax.experimental import pallas as pl
from jax.experimental.pallas import tpu as pltpu
from jax.sharding import Mesh
from jax.sharding import PartitionSpec as P


TP = ("z", "y", "c")
BF16 = jnp.bfloat16
F32 = jnp.float32
VMEM = pl.BlockSpec(memory_space=pltpu.VMEM)
HBM = pl.BlockSpec(memory_space=pltpu.HBM)
SMEM = pl.BlockSpec(memory_space=pltpu.SMEM)


def dot(a, b, ca, cb):
    return lax.dot_general(a, b, (((ca,), (cb,)), ((), ())), preferred_element_type=F32)


def product(on_real, on_imag):
    k = on_real.shape[1] // 2
    return jnp.concatenate(
        [on_real[:, :k] - on_imag[:, k:], on_real[:, k:] + on_imag[:, :k]], axis=1
    )


def columns(tau_hbm, tau_ref, sems, chunk):
    size = tau_hbm.shape[1]
    at = pl.ds(pl.multiple_of(chunk * size, size), size)
    return pltpu.make_async_copy(
        tau_hbm.at[:, :, at], tau_ref.at[:, :, at], sems.at[chunk]
    )


def add_chunk(tau_ref, tile, chunk, total):
    both = jnp.concatenate([tile[0], tile[1]], axis=1)
    size = tau_ref.shape[1]
    at = pl.ds(pl.multiple_of(chunk * size, size), size)
    added = [dot(tau_ref[c, :, at], both, 1, 0) for c in range(2)]
    return added if total is None else [x + y for x, y in zip(total, added)]


def own_kernel(
    tau_hbm, tile_hbm, lists_hbm, load_ref, total_ref, meta_ref, tau_ref, tile_ref, lists_ref, sems, small
):
    own = lax.axis_index("blk")
    copies = [
        pltpu.make_async_copy(tile_hbm, tile_ref, small.at[0]),
        pltpu.make_async_copy(lists_hbm, lists_ref, small.at[1]),
        columns(tau_hbm, tau_ref, sems, own),
    ]
    for copy in copies:
        copy.start()
    for copy in copies:
        copy.wait()
    sides, slots = lists_ref.shape
    lists = lists_ref[...].astype(F32)
    lists = jnp.concatenate([lists, jnp.zeros((sides, meta_ref.shape[1] - slots), F32)], axis=1)
    row = lax.broadcasted_iota(jnp.int32, meta_ref.shape, 0)
    meta = jnp.where(row == sides, load_ref[0], 0).astype(F32)
    for side in range(sides):
        meta = jnp.where(row == side, lists[side : side + 1], meta)
    meta_ref[...] = meta.astype(BF16)
    total_ref[0], total_ref[1] = add_chunk(tau_ref, tile_ref[...], own, None)


def legs_kernel(
    tau_hbm, beta_hbm, tile_ref, own_ref, out_hbm, tau_ref, beta_ref, out_ref, sems
):
    parts, _, rows, _ = tile_ref.shape
    own = lax.axis_index("blk")
    others = [lax.rem(own + j, parts) for j in range(1, parts)]
    for chunk in others:
        columns(tau_hbm, tau_ref, sems.at[0], chunk).start()
    beta_copies = [
        pltpu.make_async_copy(
            beta_hbm.at[:, pl.ds(j * rows, rows), :],
            beta_ref.at[:, pl.ds(j * rows, rows), :],
            sems.at[1, j],
        )
        for j in range(parts)
    ]
    for copy in beta_copies:
        copy.start()
    total = [own_ref[0], own_ref[1]]
    for chunk in others:
        columns(tau_hbm, tau_ref, sems.at[0], chunk).wait()
        total = add_chunk(tau_ref, tile_ref[chunk], chunk, total)
    image = product(*total).astype(BF16)
    out_copies = []
    for j in range(parts):
        beta_copies[j].wait()
        out_ref[j] = product(
            dot(beta_ref[0, j * rows : (j + 1) * rows, :], image, 1, 0),
            dot(beta_ref[1, j * rows : (j + 1) * rows, :], image, 1, 0),
        ).astype(BF16)
        out_copies.append(pltpu.make_async_copy(out_ref.at[j], out_hbm.at[j], sems.at[2, j]))
        out_copies[-1].start()
    for copy in out_copies:
        copy.wait()


def pack_kernel(scale, meta_ref, parts_ref, sink_ref, out_ref):
    slices = out_ref.shape[0]
    k = sink_ref.shape[2]
    dressed = parts_ref[0].astype(F32)
    for j in range(1, parts_ref.shape[0]):
        dressed = dressed + parts_ref[j].astype(F32)
    dressed = dressed.astype(BF16)
    both = product(dot(sink_ref[0], dressed, 0, 0), -dot(sink_ref[1], dressed, 0, 0)) * scale
    real, imag = both[:, :k], both[:, k:]
    cut = [x.reshape(slices, k // slices, k) for x in (real.T, imag.T, real, imag)]
    packed = jnp.concatenate(cut, axis=1).astype(BF16)
    n = packed.shape[1]
    out_ref[:, :n, :] = packed
    for j in range(slices):
        out_ref[j, n:, :] = meta_ref[...]


def sum_kernel(ny, nc, in_ref, out_ref, numbers_ref):
    copies, pairs, rows, _ = out_ref.shape
    parts = in_ref.shape[0] // pairs
    tail = numbers_ref.shape[1]
    mine = lax.axis_index("c")
    for q in range(pairs):
        total = in_ref[q * parts, :rows, :].astype(F32)
        for j in range(1, parts):
            total = total + in_ref[q * parts + j, :rows, :].astype(F32)
        total = total.astype(BF16)
        for y in range(copies):
            out_ref[y, q] = total
        raw = in_ref[q * parts, rows:, :].astype(F32).astype(jnp.int32)[:tail]
        core, rest = raw & (nc - 1), raw >> (nc.bit_length() - 1)
        y, z = rest & (ny - 1), rest >> (ny.bit_length() - 1)
        place = jnp.where(core == mine, 0, ny * pairs) + y * pairs + z
        row = lax.broadcasted_iota(jnp.int32, raw.shape, 0)
        numbers_ref[q] = jnp.where(row < 2, place, raw)


def product_kernel(slots, scale, numbers_ref, own_ref, other_ref, out_ref, both_ref):
    owners, quarters, _, rows, k = out_ref.shape
    n = own_ref.shape[0]
    w = own_ref.shape[1] // 4
    both_ref[:n] = own_ref[...]
    both_ref[n:] = other_ref[...]
    for o in range(owners):
        load = numbers_ref[o, 2, 0]
        lefts, reals, imags = [], [], []
        for g in range(slots):
            left = both_ref[numbers_ref[o, 0, g], : 2 * w, :]
            right = both_ref[numbers_ref[o, 1, g], 2 * w :, :].astype(F32)
            lefts.append(jnp.where(g < load, left, jnp.zeros_like(left)))
            reals += [right[:w], -right[w:]]
            imags += [right[w:], right[:w]]
        left = jnp.concatenate(lefts, axis=0)
        right = jnp.concatenate(
            [jnp.concatenate(reals, axis=0), jnp.concatenate(imags, axis=0)], axis=1
        ).astype(BF16)
        total = dot(left, right, 0, 0) * scale
        for q in range(quarters):
            for c in range(2):
                out_ref[o, q, c] = total[q * rows : (q + 1) * rows, c * k : (c + 1) * k].astype(BF16)


def call(kernel, outs, specs, scratch=(), flops=0, moved=0, grant=16, out=VMEM):
    outs = [jax.ShapeDtypeStruct(*out) for out in outs]
    return pl.pallas_call(
        kernel,
        out_shape=outs,
        in_specs=specs,
        out_specs=[out] * len(outs),
        scratch_shapes=scratch,
        compiler_params=pltpu.CompilerParams(vmem_limit_bytes=grant * 2**20),
        cost_estimate=pl.CostEstimate(flops=flops, bytes_accessed=moved, transcendentals=0),
    )


def on_device(perambulator, backward, elementals, diagrams, owner_loads):
    tau = pltpu.with_memory_space_constraint(perambulator[0], pltpu.HBM)
    beta = pltpu.with_memory_space_constraint(backward[0], pltpu.HBM)
    lists = pltpu.with_memory_space_constraint(diagrams[0].T, pltpu.HBM)
    tile = elementals[0, 0]
    _, share, k = tile.shape
    order = tau.shape[2]
    nx, nz, ny, nc = (lax.axis_size(a) for a in ("blk", "z", "y", "c"))
    ns = lax.axis_size("sec")
    slots = diagrams.shape[1]
    slices = nz * nx
    w = k // slices
    quarter = k // nx

    before = lax.ppermute(tile, "sec", [((i - 1) % ns, i) for i in range(ns)])
    tiles = lax.all_to_all(jnp.broadcast_to(tile[None], (nx, *tile.shape)), "blk", 0, 0, tiled=True)
    total, meta = call(
        own_kernel,
        [((2, share, 2 * k), F32), ((16, k), BF16)],
        [HBM, HBM, HBM, SMEM],
        [
            pltpu.VMEM(tau.shape, BF16),
            pltpu.VMEM(tile.shape, BF16),
            pltpu.VMEM(lists.shape, jnp.int32),
            pltpu.SemaphoreType.DMA((nx,)),
            pltpu.SemaphoreType.DMA((2,)),
        ],
        8 * k * share * share,
        2**20,
    )(tau, pltpu.with_memory_space_constraint(tile, pltpu.HBM), lists, owner_loads)
    (dressed,) = call(
        legs_kernel,
        [((nx, share, 2 * k), BF16)],
        [HBM, HBM, VMEM, VMEM],
        [
            pltpu.VMEM(tau.shape, BF16),
            pltpu.VMEM(beta.shape, BF16),
            pltpu.VMEM((nx, share, 2 * k), BF16),
            pltpu.SemaphoreType.DMA((3, nx)),
        ],
        16 * k * order * share,
        2**23,
        out=HBM,
    )(tau, beta, tiles, total)
    dressed = lax.all_to_all(dressed, "blk", 0, 0, tiled=True)
    (packed,) = call(
        lambda *refs: pack_kernel(order**-0.5, *refs), [((slices, 4 * w + 16, k), BF16)], [VMEM] * 3
    )(meta, dressed, before)
    packed = lax.all_to_all(packed, ("z", "blk"), 0, 0, tiled=True)
    pieces, numbers = call(
        lambda *refs: sum_kernel(ny, nc, *refs),
        [((ny, nz, 4 * w, k), BF16), ((nz, 8, k), jnp.int32)],
        [VMEM],
    )(packed)
    pieces = lax.all_to_all(pieces, "y", 0, 0, tiled=True)
    others = lax.ppermute(pieces, "c", [(i, (i + 1) % nc) for i in range(nc)])
    (partial,) = call(
        lambda *refs: product_kernel(slots, (k * slots) ** -0.5, *refs),
        [((nz, nx, 2, quarter, k), BF16)],
        [SMEM, VMEM, VMEM],
        [pltpu.VMEM((2 * ny * nz, 4 * w, k), BF16)],
    )(numbers, *(x.reshape(ny * nz, 4 * w, k) for x in (pieces, others)))
    arrived = lax.all_to_all(
        partial.reshape(slices, 2, quarter, k), ("z", "blk"), 0, 0, tiled=True
    )
    total = jnp.sum(arrived.astype(F32), axis=0)
    return total.reshape(1, 1, 2, quarter, k)


def solution(mesh):
    torus = Mesh(
        mesh.devices.reshape(mesh.shape["sec"], 4, 8, 2, mesh.shape["blk"]),
        ("sec", "z", "y", "c", "blk"),
    )
    in_specs = (
        P(TP, None, "blk", None),
        P(TP, None, None, "blk"),
        P("sec", TP, None, "blk", None),
        P(TP, None, None),
        P(TP),
    )
    out_specs = P("sec", TP, None, "blk", None)
    return jax.shard_map(
        on_device, mesh=torus, in_specs=in_specs, out_specs=out_specs, check_vma=False
    )
```

```python
import jax
import jax.numpy as jnp
from jax import lax
from jax.experimental import pallas as pl
from jax.experimental.pallas import tpu as pltpu
from jax.sharding import Mesh
from jax.sharding import PartitionSpec as P


TP = ("z", "y", "c")
BF16 = jnp.bfloat16
F32 = jnp.float32
VMEM = pl.BlockSpec(memory_space=pltpu.VMEM)
HBM = pl.BlockSpec(memory_space=pltpu.HBM)
SMEM = pl.BlockSpec(memory_space=pltpu.SMEM)


def dot(a, b, ca, cb):
    return lax.dot_general(a, b, (((ca,), (cb,)), ((), ())), preferred_element_type=F32)


def product(on_real, on_imag):
    k = on_real.shape[1] // 2
    return jnp.concatenate(
        [on_real[:, :k] - on_imag[:, k:], on_real[:, k:] + on_imag[:, :k]], axis=1
    )


def spread_kernel(tile_hbm, out_hbm, tile_ref, sems):
    parts = out_hbm.shape[0]
    copy = pltpu.make_async_copy(tile_hbm, tile_ref, sems.at[parts])
    copy.start()
    copy.wait()
    copies = [
        pltpu.make_async_copy(tile_ref, out_hbm.at[j], sems.at[j]) for j in range(parts)
    ]
    for copy in copies:
        copy.start()
    for copy in copies:
        copy.wait()


def columns(tau_hbm, tau_ref, sems, chunk):
    size = tau_hbm.shape[1]
    at = pl.ds(pl.multiple_of(chunk * size, size), size)
    return pltpu.make_async_copy(
        tau_hbm.at[:, :, at], tau_ref.at[:, :, at], sems.at[chunk]
    )


def add_chunk(tau_ref, tile, chunk, total):
    both = jnp.concatenate([tile[0], tile[1]], axis=1)
    size = tau_ref.shape[1]
    at = pl.ds(pl.multiple_of(chunk * size, size), size)
    added = [dot(tau_ref[c, :, at], both, 1, 0) for c in range(2)]
    return added if total is None else [x + y for x, y in zip(total, added)]


def own_kernel(
    tau_hbm,
    beta_hbm,
    tile_hbm,
    lists_hbm,
    load_ref,
    total_ref,
    beta_ref,
    meta_ref,
    tau_ref,
    tile_ref,
    lists_ref,
    sems,
    small,
):
    own = lax.axis_index("blk")
    copies = [
        pltpu.make_async_copy(tile_hbm, tile_ref, small.at[0]),
        pltpu.make_async_copy(lists_hbm, lists_ref, small.at[1]),
        columns(tau_hbm, tau_ref, sems, own),
        pltpu.make_async_copy(beta_hbm.at[:, pl.ds(0, beta_ref.shape[1]), :], beta_ref, small.at[2]),
    ]
    for copy in copies:
        copy.start()
    for copy in copies:
        copy.wait()
    sides, slots = lists_ref.shape
    lists = lists_ref[...].astype(F32)
    lists = jnp.concatenate([lists, jnp.zeros((sides, meta_ref.shape[1] - slots), F32)], axis=1)
    row = lax.broadcasted_iota(jnp.int32, meta_ref.shape, 0)
    meta = jnp.where(row == sides, load_ref[0], 0).astype(F32)
    for side in range(sides):
        meta = jnp.where(row == side, lists[side : side + 1], meta)
    meta_ref[...] = meta.astype(BF16)
    total_ref[0], total_ref[1] = add_chunk(tau_ref, tile_ref[...], own, None)


def legs_kernel(
    tau_hbm, beta_hbm, tile_ref, own_ref, first_ref, out_hbm, tau_ref, beta_ref, out_ref, sems
):
    parts, _, rows, _ = tile_ref.shape
    own = lax.axis_index("blk")
    others = [lax.rem(own + j, parts) for j in range(1, parts)]
    for chunk in others:
        columns(tau_hbm, tau_ref, sems.at[0], chunk).start()
    beta_copies = [
        pltpu.make_async_copy(
            beta_hbm.at[:, pl.ds(j * rows, rows), :], beta_ref.at[j - 1], sems.at[1, j]
        )
        for j in range(1, parts)
    ]
    total = [own_ref[0], own_ref[1]]
    for chunk, copy in zip(others, beta_copies):
        columns(tau_hbm, tau_ref, sems.at[0], chunk).wait()
        copy.start()
        total = add_chunk(tau_ref, tile_ref[chunk], chunk, total)
    image = product(*total).astype(BF16)
    out_copies = []
    for j in range(parts):
        if j > 0:
            beta_copies[j - 1].wait()
        beta = first_ref if j == 0 else beta_ref.at[j - 1]
        out_ref[j] = product(dot(beta[0], image, 1, 0), dot(beta[1], image, 1, 0)).astype(BF16)
        out_copies.append(pltpu.make_async_copy(out_ref.at[j], out_hbm.at[j], sems.at[2, j]))
        out_copies[-1].start()
    for copy in out_copies:
        copy.wait()


def pack_kernel(scale, meta_ref, parts_ref, sink_ref, out_ref):
    slices = out_ref.shape[0]
    k = sink_ref.shape[2]
    dressed = parts_ref[0].astype(F32)
    for j in range(1, parts_ref.shape[0]):
        dressed = dressed + parts_ref[j].astype(F32)
    dressed = dressed.astype(BF16)
    both = product(dot(sink_ref[0], dressed, 0, 0), -dot(sink_ref[1], dressed, 0, 0)) * scale
    real, imag = both[:, :k], both[:, k:]
    cut = [x.reshape(slices, k // slices, k) for x in (real.T, imag.T, real, imag)]
    packed = jnp.concatenate(cut, axis=1).astype(BF16)
    n = packed.shape[1]
    out_ref[:, :n, :] = packed
    for j in range(slices):
        out_ref[j, n:, :] = meta_ref[...]


def sum_kernel(ny, nc, in_ref, out_ref, numbers_ref):
    copies, pairs, rows, _ = out_ref.shape
    parts = in_ref.shape[0] // pairs
    tail = numbers_ref.shape[1]
    mine = lax.axis_index("c")
    for q in range(pairs):
        total = in_ref[q * parts, :rows, :].astype(F32)
        for j in range(1, parts):
            total = total + in_ref[q * parts + j, :rows, :].astype(F32)
        total = total.astype(BF16)
        for y in range(copies):
            out_ref[y, q] = total
        raw = in_ref[q * parts, rows:, :].astype(F32).astype(jnp.int32)[:tail]
        core, rest = raw & (nc - 1), raw >> (nc.bit_length() - 1)
        y, z = rest & (ny - 1), rest >> (ny.bit_length() - 1)
        place = jnp.where(core == mine, 0, ny * pairs) + y * pairs + z
        row = lax.broadcasted_iota(jnp.int32, raw.shape, 0)
        numbers_ref[q] = jnp.where(row < 2, place, raw)


def product_kernel(slots, scale, numbers_ref, own_ref, other_ref, out_ref, both_ref):
    owners, quarters, _, rows, k = out_ref.shape
    n = own_ref.shape[0]
    w = own_ref.shape[1] // 4
    both_ref[:n] = own_ref[...]
    both_ref[n:] = other_ref[...]
    for o in range(owners):
        load = numbers_ref[o, 2, 0]
        lefts, reals, imags = [], [], []
        for g in range(slots):
            left = both_ref[numbers_ref[o, 0, g], : 2 * w, :]
            right = both_ref[numbers_ref[o, 1, g], 2 * w :, :].astype(F32)
            lefts.append(jnp.where(g < load, left, jnp.zeros_like(left)))
            reals += [right[:w], -right[w:]]
            imags += [right[w:], right[:w]]
        left = jnp.concatenate(lefts, axis=0)
        right = jnp.concatenate(
            [jnp.concatenate(reals, axis=0), jnp.concatenate(imags, axis=0)], axis=1
        ).astype(BF16)
        total = dot(left, right, 0, 0) * scale
        for q in range(quarters):
            for c in range(2):
                out_ref[o, q, c] = total[q * rows : (q + 1) * rows, c * k : (c + 1) * k].astype(BF16)


def call(kernel, outs, specs, scratch=(), flops=0, moved=0, grant=16, out=VMEM):
    outs = [jax.ShapeDtypeStruct(*out) for out in outs]
    return pl.pallas_call(
        kernel,
        out_shape=outs,
        in_specs=specs,
        out_specs=[out] * len(outs),
        scratch_shapes=scratch,
        compiler_params=pltpu.CompilerParams(vmem_limit_bytes=grant * 2**20),
        cost_estimate=pl.CostEstimate(flops=flops, bytes_accessed=moved, transcendentals=0),
    )


def on_device(perambulator, backward, elementals, diagrams, owner_loads):
    tau = pltpu.with_memory_space_constraint(perambulator[0], pltpu.HBM)
    beta = pltpu.with_memory_space_constraint(backward[0], pltpu.HBM)
    lists = pltpu.with_memory_space_constraint(diagrams[0].T, pltpu.HBM)
    tile = elementals[0, 0]
    _, share, k = tile.shape
    order = tau.shape[2]
    nx, nz, ny, nc = (lax.axis_size(a) for a in ("blk", "z", "y", "c"))
    ns = lax.axis_size("sec")
    slots = diagrams.shape[1]
    slices = nz * nx
    w = k // slices
    quarter = k // nx

    before = lax.ppermute(tile, "sec", [((i - 1) % ns, i) for i in range(ns)])
    tile_hbm = pltpu.with_memory_space_constraint(tile, pltpu.HBM)
    (tiles,) = call(
        spread_kernel,
        [((nx, *tile.shape), BF16)],
        [HBM],
        [pltpu.VMEM(tile.shape, BF16), pltpu.SemaphoreType.DMA((nx + 1,))],
        out=HBM,
    )(tile_hbm)
    tiles = lax.all_to_all(tiles, "blk", 0, 0, tiled=True)
    total, beta_first, meta = call(
        own_kernel,
        [((2, share, 2 * k), F32), ((2, share, share), BF16), ((16, k), BF16)],
        [HBM, HBM, HBM, HBM, SMEM],
        [
            pltpu.VMEM(tau.shape, BF16),
            pltpu.VMEM(tile.shape, BF16),
            pltpu.VMEM(lists.shape, jnp.int32),
            pltpu.SemaphoreType.DMA((nx,)),
            pltpu.SemaphoreType.DMA((3,)),
        ],
        8 * k * share * share,
        2**20,
    )(tau, beta, tile_hbm, lists, owner_loads)
    (dressed,) = call(
        legs_kernel,
        [((nx, share, 2 * k), BF16)],
        [HBM, HBM, VMEM, VMEM, VMEM],
        [
            pltpu.VMEM(tau.shape, BF16),
            pltpu.VMEM((nx - 1, 2, share, share), BF16),
            pltpu.VMEM((nx, share, 2 * k), BF16),
            pltpu.SemaphoreType.DMA((3, nx)),
        ],
        16 * k * order * share,
        2**23,
        out=HBM,
    )(tau, beta, tiles, total, beta_first)
    dressed = lax.all_to_all(dressed, "blk", 0, 0, tiled=True)
    (packed,) = call(
        lambda *refs: pack_kernel(order**-0.5, *refs), [((slices, 4 * w + 16, k), BF16)], [VMEM] * 3
    )(meta, dressed, before)
    packed = lax.all_to_all(packed, ("z", "blk"), 0, 0, tiled=True)
    pieces, numbers = call(
        lambda *refs: sum_kernel(ny, nc, *refs),
        [((ny, nz, 4 * w, k), BF16), ((nz, 8, k), jnp.int32)],
        [VMEM],
    )(packed)
    pieces = lax.all_to_all(pieces, "y", 0, 0, tiled=True)
    others = lax.ppermute(pieces, "c", [(i, (i + 1) % nc) for i in range(nc)])
    (partial,) = call(
        lambda *refs: product_kernel(slots, (k * slots) ** -0.5, *refs),
        [((nz, nx, 2, quarter, k), BF16)],
        [SMEM, VMEM, VMEM],
        [pltpu.VMEM((2 * ny * nz, 4 * w, k), BF16)],
    )(numbers, *(x.reshape(ny * nz, 4 * w, k) for x in (pieces, others)))
    arrived = lax.all_to_all(
        partial.reshape(slices, 2, quarter, k), ("z", "blk"), 0, 0, tiled=True
    )
    total = jnp.sum(arrived.astype(F32), axis=0)
    return total.reshape(1, 1, 2, quarter, k)


def solution(mesh):
    torus = Mesh(
        mesh.devices.reshape(mesh.shape["sec"], 4, 8, 2, mesh.shape["blk"]),
        ("sec", "z", "y", "c", "blk"),
    )
    in_specs = (
        P(TP, None, "blk", None),
        P(TP, None, None, "blk"),
        P("sec", TP, None, "blk", None),
        P(TP, None, None),
        P(TP),
    )
    out_specs = P("sec", TP, None, "blk", None)
    return jax.shard_map(
        on_device, mesh=torus, in_specs=in_specs, out_specs=out_specs, check_vma=False
    )
```

```python
import jax
import jax.numpy as jnp
from jax import lax
from jax.experimental import pallas as pl
from jax.experimental.pallas import tpu as pltpu
from jax.sharding import Mesh
from jax.sharding import PartitionSpec as P


TP = ("z", "y", "c")
BF16 = jnp.bfloat16
F32 = jnp.float32
VMEM = pl.BlockSpec(memory_space=pltpu.VMEM)
HBM = pl.BlockSpec(memory_space=pltpu.HBM)
SMEM = pl.BlockSpec(memory_space=pltpu.SMEM)


def dot(a, b, ca, cb):
    return lax.dot_general(a, b, (((ca,), (cb,)), ((), ())), preferred_element_type=F32)


def product(on_real, on_imag):
    k = on_real.shape[1] // 2
    return jnp.concatenate(
        [on_real[:, :k] - on_imag[:, k:], on_real[:, k:] + on_imag[:, :k]], axis=1
    )


def spread_kernel(tile_hbm, out_hbm, tile_ref, sems):
    parts = out_hbm.shape[0]
    copy = pltpu.make_async_copy(tile_hbm, tile_ref, sems.at[parts])
    copy.start()
    copy.wait()
    copies = [
        pltpu.make_async_copy(tile_ref, out_hbm.at[j], sems.at[j]) for j in range(parts)
    ]
    for copy in copies:
        copy.start()
    for copy in copies:
        copy.wait()


def columns(tau_hbm, tau_ref, sems, chunk):
    size = tau_hbm.shape[1]
    at = pl.ds(pl.multiple_of(chunk * size, size), size)
    return pltpu.make_async_copy(
        tau_hbm.at[:, :, at], tau_ref.at[:, :, at], sems.at[chunk]
    )


def add_chunk(tau_ref, tile, chunk, total):
    both = jnp.concatenate([tile[0], tile[1]], axis=1)
    size = tau_ref.shape[1]
    at = pl.ds(pl.multiple_of(chunk * size, size), size)
    added = [dot(tau_ref[c, :, at], both, 1, 0) for c in range(2)]
    return added if total is None else [x + y for x, y in zip(total, added)]


def own_kernel(
    tau_hbm,
    beta_hbm,
    tile_hbm,
    lists_hbm,
    load_ref,
    total_ref,
    beta_ref,
    meta_ref,
    tau_ref,
    tile_ref,
    lists_ref,
    sems,
    small,
):
    own = lax.axis_index("blk")
    copies = [
        pltpu.make_async_copy(tile_hbm, tile_ref, small.at[0]),
        pltpu.make_async_copy(lists_hbm, lists_ref, small.at[1]),
        columns(tau_hbm, tau_ref, sems, own),
        pltpu.make_async_copy(beta_hbm.at[:, pl.ds(0, beta_ref.shape[1]), :], beta_ref, small.at[2]),
    ]
    for copy in copies:
        copy.start()
    for copy in copies:
        copy.wait()
    sides, slots = lists_ref.shape
    lists = lists_ref[...].astype(F32)
    lists = jnp.concatenate([lists, jnp.zeros((sides, meta_ref.shape[1] - slots), F32)], axis=1)
    row = lax.broadcasted_iota(jnp.int32, meta_ref.shape, 0)
    meta = jnp.where(row == sides, load_ref[0], 0).astype(F32)
    for side in range(sides):
        meta = jnp.where(row == side, lists[side : side + 1], meta)
    meta_ref[...] = meta.astype(BF16)
    total_ref[0], total_ref[1] = add_chunk(tau_ref, tile_ref[...], own, None)


def legs_kernel(
    tau_hbm, beta_hbm, tile_ref, own_ref, first_ref, out_hbm, tau_ref, beta_ref, out_ref, sems
):
    parts, _, rows, _ = tile_ref.shape
    own = lax.axis_index("blk")
    others = [lax.rem(own + j, parts) for j in range(1, parts)]
    for chunk in others:
        columns(tau_hbm, tau_ref, sems.at[0], chunk).start()
    beta_copies = [
        pltpu.make_async_copy(
            beta_hbm.at[:, pl.ds(j * rows, rows), :], beta_ref.at[j - 1], sems.at[1, j]
        )
        for j in range(1, parts)
    ]
    for copy in beta_copies:
        copy.start()
    total = [own_ref[0], own_ref[1]]
    for chunk in others:
        columns(tau_hbm, tau_ref, sems.at[0], chunk).wait()
        total = add_chunk(tau_ref, tile_ref[chunk], chunk, total)
    image = product(*total).astype(BF16)
    out_copies = []
    for j in range(parts):
        if j > 0:
            beta_copies[j - 1].wait()
        beta = first_ref if j == 0 else beta_ref.at[j - 1]
        out_ref[j] = product(dot(beta[0], image, 1, 0), dot(beta[1], image, 1, 0)).astype(BF16)
        out_copies.append(pltpu.make_async_copy(out_ref.at[j], out_hbm.at[j], sems.at[2, j]))
        out_copies[-1].start()
    for copy in out_copies:
        copy.wait()


def pack_kernel(scale, meta_ref, parts_ref, sink_ref, out_ref):
    slices = out_ref.shape[0]
    k = sink_ref.shape[2]
    dressed = parts_ref[0].astype(F32)
    for j in range(1, parts_ref.shape[0]):
        dressed = dressed + parts_ref[j].astype(F32)
    dressed = dressed.astype(BF16)
    both = product(dot(sink_ref[0], dressed, 0, 0), -dot(sink_ref[1], dressed, 0, 0)) * scale
    real, imag = both[:, :k], both[:, k:]
    cut = [x.reshape(slices, k // slices, k) for x in (real.T, imag.T, real, imag)]
    packed = jnp.concatenate(cut, axis=1).astype(BF16)
    n = packed.shape[1]
    out_ref[:, :n, :] = packed
    for j in range(slices):
        out_ref[j, n:, :] = meta_ref[...]


def sum_kernel(ny, nc, in_ref, out_ref, numbers_ref):
    copies, pairs, rows, _ = out_ref.shape
    parts = in_ref.shape[0] // pairs
    tail = numbers_ref.shape[1]
    mine = lax.axis_index("c")
    for q in range(pairs):
        total = in_ref[q * parts, :rows, :].astype(F32)
        for j in range(1, parts):
            total = total + in_ref[q * parts + j, :rows, :].astype(F32)
        total = total.astype(BF16)
        for y in range(copies):
            out_ref[y, q] = total
        raw = in_ref[q * parts, rows:, :].astype(F32).astype(jnp.int32)[:tail]
        core, rest = raw & (nc - 1), raw >> (nc.bit_length() - 1)
        y, z = rest & (ny - 1), rest >> (ny.bit_length() - 1)
        place = jnp.where(core == mine, 0, ny * pairs) + y * pairs + z
        row = lax.broadcasted_iota(jnp.int32, raw.shape, 0)
        numbers_ref[q] = jnp.where(row < 2, place, raw)


def product_kernel(slots, scale, numbers_ref, own_ref, other_ref, out_ref, both_ref):
    owners, quarters, _, rows, k = out_ref.shape
    n = own_ref.shape[0]
    w = own_ref.shape[1] // 4
    both_ref[:n] = own_ref[...]
    both_ref[n:] = other_ref[...]
    for o in range(owners):
        load = numbers_ref[o, 2, 0]
        lefts, reals, imags = [], [], []
        for g in range(slots):
            left = both_ref[numbers_ref[o, 0, g], : 2 * w, :]
            right = both_ref[numbers_ref[o, 1, g], 2 * w :, :].astype(F32)
            lefts.append(jnp.where(g < load, left, jnp.zeros_like(left)))
            reals += [right[:w], -right[w:]]
            imags += [right[w:], right[:w]]
        left = jnp.concatenate(lefts, axis=0)
        right = jnp.concatenate(
            [jnp.concatenate(reals, axis=0), jnp.concatenate(imags, axis=0)], axis=1
        ).astype(BF16)
        total = dot(left, right, 0, 0) * scale
        for q in range(quarters):
            for c in range(2):
                out_ref[o, q, c] = total[q * rows : (q + 1) * rows, c * k : (c + 1) * k].astype(BF16)


def call(kernel, outs, specs, scratch=(), flops=0, moved=0, grant=16, out=VMEM):
    outs = [jax.ShapeDtypeStruct(*out) for out in outs]
    return pl.pallas_call(
        kernel,
        out_shape=outs,
        in_specs=specs,
        out_specs=[out] * len(outs),
        scratch_shapes=scratch,
        compiler_params=pltpu.CompilerParams(vmem_limit_bytes=grant * 2**20),
        cost_estimate=pl.CostEstimate(flops=flops, bytes_accessed=moved, transcendentals=0),
    )


def on_device(perambulator, backward, elementals, diagrams, owner_loads):
    tau = pltpu.with_memory_space_constraint(perambulator[0], pltpu.HBM)
    beta = pltpu.with_memory_space_constraint(backward[0], pltpu.HBM)
    lists = pltpu.with_memory_space_constraint(diagrams[0].T, pltpu.HBM)
    tile = elementals[0, 0]
    _, share, k = tile.shape
    order = tau.shape[2]
    nx, nz, ny, nc = (lax.axis_size(a) for a in ("blk", "z", "y", "c"))
    ns = lax.axis_size("sec")
    slots = diagrams.shape[1]
    slices = nz * nx
    w = k // slices
    quarter = k // nx

    before = lax.ppermute(tile, "sec", [((i - 1) % ns, i) for i in range(ns)])
    tile_hbm = pltpu.with_memory_space_constraint(tile, pltpu.HBM)
    (tiles,) = call(
        spread_kernel,
        [((nx, *tile.shape), BF16)],
        [HBM],
        [pltpu.VMEM(tile.shape, BF16), pltpu.SemaphoreType.DMA((nx + 1,))],
        out=HBM,
    )(tile_hbm)
    tiles = lax.all_to_all(tiles, "blk", 0, 0, tiled=True)
    total, beta_first, meta = call(
        own_kernel,
        [((2, share, 2 * k), F32), ((2, share, share), BF16), ((8, k), BF16)],
        [HBM, HBM, HBM, HBM, SMEM],
        [
            pltpu.VMEM(tau.shape, BF16),
            pltpu.VMEM(tile.shape, BF16),
            pltpu.VMEM(lists.shape, jnp.int32),
            pltpu.SemaphoreType.DMA((nx,)),
            pltpu.SemaphoreType.DMA((3,)),
        ],
        8 * k * share * share,
        2**20,
    )(tau, beta, tile_hbm, lists, owner_loads)
    (dressed,) = call(
        legs_kernel,
        [((nx, share, 2 * k), BF16)],
        [HBM, HBM, VMEM, VMEM, VMEM],
        [
            pltpu.VMEM(tau.shape, BF16),
            pltpu.VMEM((nx - 1, 2, share, share), BF16),
            pltpu.VMEM((nx, share, 2 * k), BF16),
            pltpu.SemaphoreType.DMA((3, nx)),
        ],
        16 * k * order * share,
        2**23,
        out=HBM,
    )(tau, beta, tiles, total, beta_first)
    dressed = lax.all_to_all(dressed, "blk", 0, 0, tiled=True)
    (packed,) = call(
        lambda *refs: pack_kernel(order**-0.5, *refs), [((slices, 4 * w + 8, k), BF16)], [VMEM] * 3
    )(meta, dressed, before)
    packed = lax.all_to_all(packed, ("z", "blk"), 0, 0, tiled=True)
    pieces, numbers = call(
        lambda *refs: sum_kernel(ny, nc, *refs),
        [((ny, nz, 4 * w, k), BF16), ((nz, 8, k), jnp.int32)],
        [VMEM],
    )(packed)
    pieces = lax.all_to_all(pieces, "y", 0, 0, tiled=True)
    others = lax.ppermute(pieces, "c", [(i, (i + 1) % nc) for i in range(nc)])
    (partial,) = call(
        lambda *refs: product_kernel(slots, (k * slots) ** -0.5, *refs),
        [((nz, nx, 2, quarter, k), BF16)],
        [SMEM, VMEM, VMEM],
        [pltpu.VMEM((2 * ny * nz, 4 * w, k), BF16)],
    )(numbers, *(x.reshape(ny * nz, 4 * w, k) for x in (pieces, others)))
    arrived = lax.all_to_all(
        partial.reshape(slices, 2, quarter, k), ("z", "blk"), 0, 0, tiled=True
    )
    total = jnp.sum(arrived.astype(F32), axis=0)
    return total.reshape(1, 1, 2, quarter, k)


def solution(mesh):
    torus = Mesh(
        mesh.devices.reshape(mesh.shape["sec"], 4, 8, 2, mesh.shape["blk"]),
        ("sec", "z", "y", "c", "blk"),
    )
    in_specs = (
        P(TP, None, "blk", None),
        P(TP, None, None, "blk"),
        P("sec", TP, None, "blk", None),
        P(TP, None, None),
        P(TP),
    )
    out_specs = P("sec", TP, None, "blk", None)
    return jax.shard_map(
        on_device, mesh=torus, in_specs=in_specs, out_specs=out_specs, check_vma=False
    )
```
